512 devices in a mesh: row: 32 (over z, x_lo, core), col: 16 (over x_hi, y).
Axes of the slice: x: 4 (x_hi: 2, x_lo: 2; x = x_hi * 2 + x_lo), y: 8, z: 8, core: 2. Of those that a mesh axis runs over, the one named last changes fastest.
Arguments:
- slab_block: bfloat16 [65536, 2048], P('row', 'col'), may hold values from -6 to 6
- scale_first: bfloat16 [65536], P('row'), may hold values from 0.5 to 2
- scale_second: bfloat16 [65536], P('row'), may hold values from 0.5 to 2
- panel_lower: bfloat16 [65536, 4096], P('row', 'col'), may hold values from -0.09375 to 0.09375
Outputs:
- updated_slab: bfloat16 [65536, 2048], P('row', 'col')
The draws below stay inside these ranges and needn't reach their ends.
All inputs are finite; a program needn't handle non-finite values.
Results may differ from the reference program's by a relative error of at most 0.015.
Values may be sent and summed in bfloat16 or wider, within the bound.
No kernel may reach another device: no remote copies, remote signals or barrier semaphores. Data moves between devices by JAX's collectives and lax.ppermute only.
A program may use at most 64 MiB of HBM per device.

```python
import math
import jax
import jax.numpy as jnp
from jax import lax

SLAB_W = 2048
PANEL_W = 4096
ROWS_DEV = 2048
ORDER = 65536
N_ROW = 32
N_COL = 16


def level_of(own_key, shape, cuts, low, top_value):
    def one(position, blocks):
        steps = jax.random.uniform(jax.random.fold_in(jax.random.fold_in(own_key, 6), position), (blocks,), jnp.float32, low / len(cuts), top_value / len(cuts))
        return jnp.repeat(jnp.exp(steps), shape[position] // blocks).reshape((-1,) + (1,) * (len(shape) - position - 1))

    factor_of = one(*cuts[0])
    for cut in cuts[1:]:
        factor_of = factor_of * one(*cut)
    return factor_of


def normal_values(key, extent, scale, most, cuts=(), dtype=jnp.bfloat16):
    factor_of = level_of(key, extent, cuts, -0.22, 0.18) if cuts else 1.0
    values = jax.random.normal(key, extent, jnp.float32) * scale * factor_of
    return jnp.minimum(jnp.maximum(values, -most), most).astype(dtype)


def setup_inputs(seed: int = 0) -> dict:
    seeds = jax.random.split(jax.random.key(seed), 5)
    return {
        "slab_block": normal_values(seeds[0], (ORDER, SLAB_W), 1.0, 6.0, ((0, 32), (1, 16))),
        "scale_first": jnp.clip(jnp.exp(math.log(2.0) - 1.3862944 * jax.random.uniform(seeds[1], (ORDER,), jnp.float32) ** level_of(seeds[1], (ORDER,), ((0, 32),), -0.2, 0.2)), 0.5, 2.0).astype(jnp.bfloat16),
        "scale_second": jnp.clip(jnp.exp(math.log(2.0) - 1.3862944 * jax.random.uniform(seeds[2], (ORDER,), jnp.float32) ** level_of(seeds[2], (ORDER,), ((0, 32),), -0.2, 0.2)), 0.5, 2.0).astype(jnp.bfloat16),
        "panel_lower": normal_values(seeds[3], (ORDER, PANEL_W), PANEL_W ** -0.5, 0.09375, ((0, 32), (1, 16))),
    }


inv_root = 0.7071067811865476


def reference(slab_block, scale_first, scale_second, panel_lower):
    first = (scale_first.astype(jnp.float32)[:, None] * slab_block.astype(jnp.float32)).astype(jnp.bfloat16)
    first = lax.optimization_barrier(first).astype(jnp.float32)
    half_rows = ORDER // 2
    upper_half = first[:half_rows]
    lower_half = first[half_rows:]
    level_one = jnp.concatenate([(upper_half + lower_half) * inv_root, (upper_half - lower_half) * inv_root], axis=0)
    second = (scale_second.astype(jnp.float32)[:, None] * level_one).astype(jnp.bfloat16)
    second = lax.optimization_barrier(second).astype(jnp.float32)
    quads = second.reshape(2, 2, ORDER // 4, SLAB_W)
    level_two = jnp.stack([(quads[:, 0] + quads[:, 1]) * inv_root, (quads[:, 0] - quads[:, 1]) * inv_root], axis=1)
    transformed = level_two.reshape(ORDER, SLAB_W).astype(jnp.bfloat16)
    stored = transformed.reshape(ROWS_DEV, N_ROW, SLAB_W).transpose(1, 0, 2).reshape(ORDER, SLAB_W)
    upper_rows = transformed[:PANEL_W]
    block_width = PANEL_W // N_COL
    update_sum = jnp.zeros((ORDER, SLAB_W), jnp.float32)
    for blocknum in range(N_COL):
        term = jnp.dot(panel_lower[:, blocknum * block_width:(blocknum + 1) * block_width],
                       upper_rows[blocknum * block_width:(blocknum + 1) * block_width],
                       preferred_element_type=jnp.float32).astype(jnp.bfloat16)
        term = lax.optimization_barrier(term)
        update_sum = update_sum + term.astype(jnp.float32)
    return (stored.astype(jnp.float32) - update_sum).astype(jnp.bfloat16)
```

```python
import jax
import jax.numpy as jnp
from jax import lax
from jax.sharding import Mesh, PartitionSpec as P

PANEL_W = 4096
X_HI = 2
CHUNKS = 4

inv_root = 0.7071067811865476


def butterfly(top, bottom):
    top = top.astype(jnp.float32)
    bottom = bottom.astype(jnp.float32)
    return jnp.concatenate([(top + bottom) * inv_root, (top - bottom) * inv_root], axis=0)


def per_device(slab_block, scale_first, scale_second, panel_lower):
    row_count, col_width = slab_block.shape
    groups = lax.axis_size("row")
    y_count = lax.axis_size("y")
    block_width = panel_lower.shape[1]
    chunk = row_count // CHUNKS

    gathered = [
        lax.all_gather(panel_lower[c * chunk : (c + 1) * chunk], "y", axis=1, tiled=True)
        for c in range(CHUNKS)
    ]

    first = (scale_first.astype(jnp.float32)[:, None] * slab_block.astype(jnp.float32)).astype(
        jnp.bfloat16
    )
    cyclic = lax.all_to_all(
        first.reshape(row_count // groups, groups, col_width), "row", split_axis=1, concat_axis=0, tiled=True
    ).reshape(row_count, col_width)
    scale_cyclic = lax.all_to_all(
        scale_second.reshape(row_count // groups, groups), "row", split_axis=1, concat_axis=0, tiled=True
    ).reshape(row_count)

    half = row_count // 2
    quarter = row_count // 4
    level_one = butterfly(cyclic[:half], cyclic[half:])
    second = (scale_cyclic.astype(jnp.float32)[:, None] * level_one).astype(jnp.bfloat16)
    stored = jnp.concatenate(
        [
            butterfly(second[:quarter], second[quarter:half]),
            butterfly(second[half : half + quarter], second[half + quarter :]),
        ],
        axis=0,
    ).astype(jnp.bfloat16)

    top_count = PANEL_W // groups // X_HI
    top = stored[: top_count * X_HI].reshape(1, X_HI, top_count, col_width)
    send = jnp.broadcast_to(top, (groups, X_HI, top_count, col_width)).reshape(
        groups * X_HI, top_count, col_width
    )
    got = lax.all_to_all(send, ("row", "x_hi"), split_axis=0, concat_axis=0)
    got = got.reshape(groups, X_HI, top_count, col_width)
    upper = jnp.transpose(got, (1, 2, 0, 3)).reshape(X_HI, top_count * groups, col_width)
    mine = lax.axis_index("x_hi")
    upper_own = lax.dynamic_index_in_dim(upper, mine, 0, keepdims=False)
    upper_far = lax.dynamic_index_in_dim(upper, 1 - mine, 0, keepdims=False)

    swap = [(i, X_HI - 1 - i) for i in range(X_HI)]
    out = []
    for c in range(CHUNKS):
        far = jnp.dot(gathered[c], upper_far, preferred_element_type=jnp.float32).astype(jnp.bfloat16)
        came = lax.ppermute(far, "x_hi", swap)
        own = jnp.dot(gathered[c], upper_own, preferred_element_type=jnp.float32)
        base = stored[c * chunk : (c + 1) * chunk].astype(jnp.float32)
        out.append((base - (own + came.astype(jnp.float32))).astype(jnp.bfloat16))
    return jnp.concatenate(out, axis=0)


def solution(mesh):
    rows, cols = mesh.devices.shape
    split = Mesh(mesh.devices.reshape(rows, X_HI, cols // X_HI), ("row", "x_hi", "y"))
    col = ("x_hi", "y")
    placed = (P("row", col), P("row"), P("row"), P("row", col))
    return jax.shard_map(
        per_device, mesh=split, in_specs=placed, out_specs=P("row", col), check_vma=False
    )
```

```python
import jax
import jax.numpy as jnp
from jax import lax
from jax.experimental import pallas as pl
from jax.experimental.pallas import tpu as pltpu
from jax.sharding import Mesh, PartitionSpec as P

PANEL_W = 4096
X_HI = 2
PAD = 8
TILE_M = 256

inv_root = 0.7071067811865476


def butterfly(top, bottom):
    top = top.astype(jnp.float32)
    bottom = bottom.astype(jnp.float32)
    return jnp.concatenate([(top + bottom) * inv_root, (top - bottom) * inv_root], axis=0)


def product_body(offsets, place_ref, upper_ref, stored_ref, *refs):
    blocks, (far_ref, rest_ref) = refs[:-2], refs[-2:]
    y_count = upper_ref.shape[0]
    total = jnp.zeros((blocks[0].shape[0], upper_ref.shape[2]), jnp.float32)
    for offset, block in zip(offsets, blocks):
        rows = upper_ref[(place_ref[1] + offset + y_count) % y_count]
        total += jnp.dot(block[...], rows, preferred_element_type=jnp.float32)
    width = far_ref.shape[1]
    left, right = total[:, :width], total[:, width:]
    at_left = place_ref[0] == 0
    far_ref[...] = jnp.where(at_left, right, left).astype(far_ref.dtype)
    rest_ref[...] = stored_ref[...].astype(jnp.float32) - jnp.where(at_left, left, right)


def products(place, upper, stored, blocks):
    offsets = tuple(offset for offset, _ in blocks)
    rows, depth = blocks[0][1].shape
    width = stored.shape[1]
    tile = lambda i, place: (i, 0)
    return pl.pallas_call(
        lambda *refs: product_body(offsets, *refs),
        grid_spec=pltpu.PrefetchScalarGridSpec(
            num_scalar_prefetch=1,
            grid=(rows // TILE_M,),
            in_specs=[
                pl.BlockSpec(upper.shape, lambda i, place: (0, 0, 0)),
                pl.BlockSpec((TILE_M, width), tile),
                *[pl.BlockSpec((TILE_M, depth), tile) for _ in blocks],
            ],
            out_specs=[pl.BlockSpec((TILE_M, width), tile), pl.BlockSpec((TILE_M, width), tile)],
        ),
        out_shape=[
            jax.ShapeDtypeStruct((rows, width), jnp.bfloat16),
            jax.ShapeDtypeStruct((rows, width), jnp.float32),
        ],
        name="products",
    )(place, upper, stored, *[block for _, block in blocks])


def per_device(slab_block, scale_first, scale_second, panel_lower):
    row_count, col_width = slab_block.shape
    groups = lax.axis_size("row")
    y_count = lax.axis_size("y")
    block_width = panel_lower.shape[1]
    share = row_count // groups
    half = row_count // 2
    quarter = row_count // 4

    up = [(i, (i + 1) % y_count) for i in range(y_count)]
    down = [(i, (i - 1) % y_count) for i in range(y_count)]
    halves = [panel_lower[:half], panel_lower[half:]]
    held = [[(0, halves[0])], [(0, halves[1])]]
    moving = {(0, -1): halves[0], (1, 1): halves[1], (1, -1): halves[1], (0, 1): halves[0]}
    steps = []
    for distance in range(1, y_count // 2 + 1):
        last = 2 * distance == y_count
        keys = ((0, -1), (1, 1)) if last else tuple(moving)
        for part, sign in keys:
            moving[part, sign] = lax.ppermute(moving[part, sign], "y", up if sign < 0 else down)
        steps.append({key: moving[key] for key in keys})

    first = (scale_first.astype(jnp.float32)[:, None] * slab_block.astype(jnp.float32)).astype(
        jnp.bfloat16
    )
    scale_rows = jnp.pad(
        jnp.transpose(scale_second.reshape(share, groups))[None], ((0, PAD - 1), (0, 0), (0, col_width - share))
    )
    packed = jnp.concatenate([first.reshape(share, groups, col_width), scale_rows], axis=0)
    packed = lax.all_to_all(packed, "row", split_axis=1, concat_axis=0, tiled=True)
    packed, steps[0] = lax.optimization_barrier((packed, steps[0]))
    packed = packed.reshape(groups, share + PAD, col_width)
    cyclic = packed[:, :share].reshape(row_count, col_width)
    scale_cyclic = packed[:, share, :share].reshape(row_count)

    level_one = butterfly(cyclic[:half], cyclic[half:])
    second = (scale_cyclic.astype(jnp.float32)[:, None] * level_one).astype(jnp.bfloat16)
    stored = jnp.concatenate(
        [
            butterfly(second[:quarter], second[quarter:half]),
            butterfly(second[half : half + quarter], second[half + quarter :]),
        ],
        axis=0,
    ).astype(jnp.bfloat16)

    top_count = PANEL_W // groups // X_HI
    top = stored[: top_count * X_HI].reshape(1, X_HI, top_count, col_width)
    send = jnp.broadcast_to(top, (groups, X_HI, top_count, col_width)).reshape(
        groups * X_HI, top_count, col_width
    )
    got = lax.all_to_all(send, ("row", "x_hi"), split_axis=0, concat_axis=0)
    got, steps[1], steps[2] = lax.optimization_barrier((got, steps[1], steps[2]))
    got = got.reshape(groups, X_HI, top_count, col_width)
    upper = jnp.transpose(got, (2, 0, 1, 3)).reshape(y_count, block_width, X_HI * col_width)

    for distance, step in enumerate(steps, 1):
        for (part, sign), block in step.items():
            held[part].append((sign * distance, block))

    place = jnp.stack([lax.axis_index("x_hi"), lax.axis_index("y")]).astype(jnp.int32)
    swap = [(i, X_HI - 1 - i) for i in range(X_HI)]
    out = []
    for part in range(2):
        far, rest = products(place, upper, stored[part * half : (part + 1) * half], held[part])
        came = lax.ppermute(far, "x_hi", swap)
        out.append((rest - came.astype(jnp.float32)).astype(jnp.bfloat16))
    return jnp.concatenate(out, axis=0)


def solution(mesh):
    rows, cols = mesh.devices.shape
    split = Mesh(mesh.devices.reshape(rows, X_HI, cols // X_HI), ("row", "x_hi", "y"))
    col = ("x_hi", "y")
    placed = (P("row", col), P("row"), P("row"), P("row", col))
    return jax.shard_map(
        per_device, mesh=split, in_specs=placed, out_specs=P("row", col), check_vma=False
    )
```

```python
import jax
import jax.numpy as jnp
from jax import lax
from jax.experimental import pallas as pl
from jax.experimental.pallas import tpu as pltpu
from jax.sharding import Mesh, PartitionSpec as P

PANEL_W = 4096
X_HI = 2
CORES = 2
PAD = 8
TILE_M = 256
ROW = ("chip", "core")

inv_root = 0.7071067811865476


def butterfly(top, bottom):
    top = top.astype(jnp.float32)
    bottom = bottom.astype(jnp.float32)
    return jnp.concatenate([(top + bottom) * inv_root, (top - bottom) * inv_root], axis=0)


def after(value, *others):
    return lax.optimization_barrier((value, *others))[0]


def load_tiles(refs, split, tiles):
    in_first = pl.program_id(0) < tiles // 2
    out, refs = [], list(refs)
    for halves in split:
        if halves:
            first, second = refs.pop(0), refs.pop(0)
            out.append(jnp.where(in_first, first[...], second[...]))
        else:
            out.append(refs.pop(0)[...])
    return out


def block_specs(blocks, tiles):
    specs, flat, split = [], [], []
    for block in blocks:
        if isinstance(block, tuple):
            shape = (TILE_M, block[0].shape[1])
            specs.append(pl.BlockSpec(shape, lambda i, place: (jnp.minimum(i, tiles // 2 - 1), 0)))
            specs.append(pl.BlockSpec(shape, lambda i, place: (jnp.maximum(i - tiles // 2, 0), 0)))
            flat += block
        else:
            specs.append(pl.BlockSpec((TILE_M, block.shape[1]), lambda i, place: (i, 0)))
            flat.append(block)
        split.append(isinstance(block, tuple))
    return specs, flat, split


def early_products(place, upper, stored, offsets, blocks):
    rows, width = stored.shape
    y_count, depth, both = upper.shape
    tiles = rows // TILE_M
    specs, flat, split = block_specs(blocks, tiles)
    tile = pl.BlockSpec((TILE_M, width), lambda i, place: (i, 0))

    def body(place_ref, upper_ref, stored_ref, *refs):
        *block_refs, far_ref, rest_ref, turned = refs

        @pl.when(pl.program_id(0) == 0)
        def _():
            for n, offset in enumerate(offsets):
                turned[n * depth : (n + 1) * depth] = upper_ref[(place_ref[1] + offset + y_count) % y_count]

        lhs = jnp.concatenate(load_tiles(block_refs, split, tiles), axis=1)
        total = jnp.dot(lhs, turned[...], preferred_element_type=jnp.float32)
        left, right = total[:, :width], total[:, width:]
        at_left = place_ref[0] == 0
        far_ref[...] = jnp.where(at_left, right, left)
        rest_ref[...] = stored_ref[...].astype(jnp.float32) - jnp.where(at_left, left, right)

    return pl.pallas_call(
        body,
        grid_spec=pltpu.PrefetchScalarGridSpec(
            num_scalar_prefetch=1,
            grid=(tiles,),
            in_specs=[pl.BlockSpec(upper.shape, lambda i, place: (0, 0, 0)), tile, *specs],
            out_specs=[tile, tile],
            scratch_shapes=[pltpu.VMEM((len(offsets) * depth, both), upper.dtype)],
        ),
        out_shape=[jax.ShapeDtypeStruct((rows, width), jnp.float32)] * 2,
        name="early_products",
    )(place, upper, stored, *flat)


def last_product(place, upper, base, block, partner, out_dtype, sign):
    rows, width = base.shape
    y_count, depth, both = upper.shape
    tiles = rows // TILE_M
    specs, flat, split = block_specs([block], tiles)
    tile = pl.BlockSpec((TILE_M, width), lambda i, place: (i, 0))

    def body(place_ref, upper_ref, base_ref, *refs):
        *block_refs, out_ref = refs
        (lhs,) = load_tiles(block_refs, split, tiles)
        term = jnp.dot(lhs, upper_ref[0], preferred_element_type=jnp.float32)
        out_ref[...] = (base_ref[...] + sign * term).astype(out_ref.dtype)

    def upper_map(i, place):
        side = 1 - place[0] if partner else place[0]
        return ((place[1] + y_count // 2) % y_count, 0, side)

    return pl.pallas_call(
        body,
        grid_spec=pltpu.PrefetchScalarGridSpec(
            num_scalar_prefetch=1,
            grid=(tiles,),
            in_specs=[pl.BlockSpec((1, depth, width), upper_map), tile, *specs],
            out_specs=tile,
        ),
        out_shape=jax.ShapeDtypeStruct((rows, width), out_dtype),
        name="last_far" if partner else "last_own",
    )(place, upper, base, *flat)


def per_device(slab_block, scale_first, scale_second, panel_lower):
    row_count, col_width = slab_block.shape
    chips = lax.axis_size("chip")
    groups = chips * CORES
    y_count = lax.axis_size("y")
    block_width = panel_lower.shape[1]
    share = row_count // groups
    half = row_count // 2
    quarter = row_count // 4

    up = [(i, (i + 1) % y_count) for i in range(y_count)]
    down = [(i, (i - 1) % y_count) for i in range(y_count)]
    route = {-1: up, 1: down}
    near = tuple(lax.ppermute(panel_lower, "y", route[sign]) for sign in route)

    first = (scale_first.astype(jnp.float32)[:, None] * slab_block.astype(jnp.float32)).astype(
        jnp.bfloat16
    )
    scale_rows = jnp.pad(
        jnp.transpose(scale_second.reshape(share, groups))[None], ((0, PAD - 1), (0, 0), (0, col_width - share))
    )
    packed = jnp.concatenate([first.reshape(share, groups, col_width), scale_rows], axis=0)
    packed = lax.all_to_all(packed, ROW, split_axis=1, concat_axis=0, tiled=True)
    moving = {}
    for part, sign in ((0, -1), (1, 1), (1, -1), (0, 1)):
        source = near[0] if sign < 0 else near[1]
        moving[part, sign] = source[part * half : (part + 1) * half]
    packed = after(packed, *moving.values())
    packed = packed.reshape(groups, share + PAD, col_width)
    cyclic = packed[:, :share].reshape(row_count, col_width)
    scale_cyclic = packed[:, share, :share].reshape(row_count)

    steps = []
    for distance in range(2, y_count // 2 + 1):
        for part, sign in ((0, -1), (1, 1)) if 2 * distance == y_count else ((0, -1), (1, 1), (1, -1), (0, 1)):
            moving[part, sign] = lax.ppermute(moving[part, sign], "y", route[sign])
        steps.append(dict(moving))

    level_one = butterfly(cyclic[:half], cyclic[half:])
    second = (scale_cyclic.astype(jnp.float32)[:, None] * level_one).astype(jnp.bfloat16)
    stored = jnp.concatenate(
        [
            butterfly(second[:quarter], second[quarter:half]),
            butterfly(second[half : half + quarter], second[half + quarter :]),
        ],
        axis=0,
    ).astype(jnp.bfloat16)

    top_count = PANEL_W // groups // X_HI
    top = stored[: top_count * X_HI].reshape(1, X_HI, top_count, col_width)
    send = jnp.broadcast_to(top, (chips, X_HI, top_count, col_width)).reshape(
        chips * X_HI, top_count, col_width
    )
    send = after(send, steps[0][0, -1], steps[0][1, 1])
    got = lax.all_to_all(send, ("chip", "x_hi"), split_axis=0, concat_axis=0)
    twin = lax.ppermute(got, "core", [(0, 1), (1, 0)])
    core_zero = lax.axis_index("core") == 0
    upper = jnp.stack([jnp.where(core_zero, got, twin), jnp.where(core_zero, twin, got)])
    upper = upper.reshape(CORES, chips, X_HI, top_count, col_width)
    upper = jnp.transpose(upper, (3, 1, 0, 2, 4)).reshape(y_count, block_width, X_HI * col_width)
    upper = after(upper, *steps[0].values(), *steps[1].values())

    place = jnp.stack([lax.axis_index("x_hi"), lax.axis_index("y")]).astype(jnp.int32)
    offsets, blocks = [0, -1, 1], [panel_lower, *near]
    for distance, step in enumerate(steps[:-1], 2):
        for sign in route:
            offsets.append(sign * distance)
            blocks.append((step[0, sign], step[1, sign]))
    last = (steps[-1][0, -1], steps[-1][1, 1])
    far, rest = early_products(place, upper, stored, offsets, blocks)
    far = last_product(place, upper, far, last, True, jnp.bfloat16, 1)
    came = lax.ppermute(far, "x_hi", [(i, X_HI - 1 - i) for i in range(X_HI)])
    rest = last_product(place, upper, rest, last, False, jnp.float32, -1)
    return (rest - came.astype(jnp.float32)).astype(jnp.bfloat16)


def solution(mesh):
    rows, cols = mesh.devices.shape
    split = Mesh(
        mesh.devices.reshape(rows // CORES, CORES, X_HI, cols // X_HI), ("chip", "core", "x_hi", "y")
    )
    col = ("x_hi", "y")
    placed = (P(ROW, col), P(ROW), P(ROW), P(ROW, col))
    return jax.shard_map(
        per_device, mesh=split, in_specs=placed, out_specs=P(ROW, col), check_vma=False
    )
```

```python
import jax
import jax.numpy as jnp
from jax import lax
from jax.experimental import pallas as pl
from jax.experimental.pallas import tpu as pltpu
from jax.sharding import Mesh, PartitionSpec as P

PANEL_W = 4096
X_HI = 2
CORES = 2
PAD = 8
TILE_M = 256
ROW = ("chip", "core")

inv_root = 0.7071067811865476


def butterfly(top, bottom):
    top = top.astype(jnp.float32)
    bottom = bottom.astype(jnp.float32)
    return jnp.concatenate([(top + bottom) * inv_root, (top - bottom) * inv_root], axis=0)


def after(value, *others):
    return lax.optimization_barrier((value, *others))[0]


VM = pltpu.VMEM


def grant(mib):
    return pltpu.CompilerParams(vmem_limit_bytes=mib << 20)


def whole():
    return pl.BlockSpec(memory_space=VM)


def order_upper(core, got, twin, y_count):
    pairs, top, width = got.shape
    chips = pairs // X_HI
    low = top // y_count
    depth = CORES * chips * low

    def body(core_ref, got_ref, twin_ref, out_ref):
        want = lax.broadcasted_iota(jnp.int32, (depth, depth), 0)
        have = lax.broadcasted_iota(jnp.int32, (depth, depth), 1)
        side = (want % CORES + core_ref[0]) % CORES
        source = side * (chips * low) + want // CORES % chips * low + want // (CORES * chips)
        move = jnp.where(source == have, 1.0, 0.0).astype(got.dtype)
        for y in range(y_count):
            for x in range(X_HI):
                pick = [
                    ref[chip * X_HI + x, y * low : (y + 1) * low] for ref in (got_ref, twin_ref) for chip in range(chips)
                ]
                rows = jnp.dot(move, jnp.concatenate(pick, axis=0), preferred_element_type=jnp.float32)
                out_ref[y, :, x * width : (x + 1) * width] = rows.astype(got.dtype)

    return pl.pallas_call(
        body,
        in_specs=[pl.BlockSpec(memory_space=pltpu.SMEM), whole(), whole()],
        out_specs=whole(),
        out_shape=jax.ShapeDtypeStruct((y_count, depth, X_HI * width), got.dtype),
        compiler_params=grant(8),
        name="order_upper",
    )(core, got, twin)


def early_products(place, upper, stored, offsets, blocks):
    rows, width = stored.shape
    y_count, depth, both = upper.shape

    def body(place_ref, upper_ref, stored_ref, *refs):
        *block_refs, far_ref, rest_ref, turned = refs
        for n, offset in enumerate(offsets):
            turned[n * depth : (n + 1) * depth] = upper_ref[(place_ref[1] + offset + y_count) % y_count]
        at_left = place_ref[0] == 0

        def one(i, carry):
            part = pl.ds(pl.multiple_of(i * TILE_M, TILE_M), TILE_M)
            lhs = jnp.concatenate([ref[part] for ref in block_refs], axis=1)
            total = jnp.dot(lhs, turned[...], preferred_element_type=jnp.float32)
            left, right = total[:, :width], total[:, width:]
            far_ref[part] = jnp.where(at_left, right, left)
            rest_ref[part] = stored_ref[part].astype(jnp.float32) - jnp.where(at_left, left, right)
            return carry

        lax.fori_loop(0, rows // TILE_M, one, 0)

    return pl.pallas_call(
        body,
        in_specs=[pl.BlockSpec(memory_space=pltpu.SMEM)] + [whole()] * (2 + len(blocks)),
        out_specs=[whole(), whole()],
        out_shape=[jax.ShapeDtypeStruct((rows, width), jnp.float32)] * 2,
        scratch_shapes=[VM((len(offsets) * depth, both), upper.dtype)],
        compiler_params=grant(16),
        name="early_products",
    )(place, upper, stored, *blocks)


def last_product(place, upper, base, halves, partner, out_dtype, sign):
    rows, width = base.shape
    y_count, depth, both = upper.shape
    half = rows // len(halves)

    def body(place_ref, upper_ref, base_ref, *refs):
        *half_refs, out_ref = refs
        side = (place_ref[0] + 1) % X_HI if partner else place_ref[0]
        columns = upper_ref[(place_ref[1] + y_count // 2) % y_count]
        columns = jnp.where(side == 0, columns[:, :width], columns[:, width:])
        for n, ref in enumerate(half_refs):
            for start in range(0, half, TILE_M):
                part = slice(n * half + start, n * half + start + TILE_M)
                term = jnp.dot(ref[start : start + TILE_M], columns, preferred_element_type=jnp.float32)
                out_ref[part] = (base_ref[part] + sign * term).astype(out_ref.dtype)

    return pl.pallas_call(
        body,
        in_specs=[pl.BlockSpec(memory_space=pltpu.SMEM)] + [whole()] * (2 + len(halves)),
        out_specs=whole(),
        out_shape=jax.ShapeDtypeStruct((rows, width), out_dtype),
        compiler_params=grant(8),
        name="last_far" if partner else "last_own",
    )(place, upper, base, *halves)


def per_device(slab_block, scale_first, scale_second, panel_lower):
    row_count, col_width = slab_block.shape
    chips = lax.axis_size("chip")
    groups = chips * CORES
    y_count = lax.axis_size("y")
    block_width = panel_lower.shape[1]
    share = row_count // groups
    half = row_count // 2
    quarter = row_count // 4

    up = [(i, (i + 1) % y_count) for i in range(y_count)]
    down = [(i, (i - 1) % y_count) for i in range(y_count)]
    route = {-1: up, 1: down}
    near = tuple(lax.ppermute(panel_lower, "y", route[sign]) for sign in route)

    first = (scale_first.astype(jnp.float32)[:, None] * slab_block.astype(jnp.float32)).astype(
        jnp.bfloat16
    )
    scale_rows = jnp.pad(
        jnp.transpose(scale_second.reshape(share, groups))[None], ((0, PAD - 1), (0, 0), (0, col_width - share))
    )
    packed = jnp.concatenate([first.reshape(share, groups, col_width), scale_rows], axis=0)
    packed = lax.all_to_all(packed, ROW, split_axis=1, concat_axis=0, tiled=True)
    packed = after(packed, *near)
    packed = packed.reshape(groups, share + PAD, col_width)
    cyclic = packed[:, :share].reshape(row_count, col_width)
    scale_cyclic = packed[:, share, :share].reshape(row_count)

    steps, moving = [near], near
    for distance in range(2, y_count // 2):
        moving = tuple(lax.ppermute(block, "y", route[sign]) for block, sign in zip(moving, route))
        steps.append(moving)
    last = (lax.ppermute(moving[0][:half], "y", up), lax.ppermute(moving[1][half:], "y", down))

    level_one = butterfly(cyclic[:half], cyclic[half:])
    second = (scale_cyclic.astype(jnp.float32)[:, None] * level_one).astype(jnp.bfloat16)
    stored = jnp.concatenate(
        [
            butterfly(second[:quarter], second[quarter:half]),
            butterfly(second[half : half + quarter], second[half + quarter :]),
        ],
        axis=0,
    ).astype(jnp.bfloat16)

    top_count = PANEL_W // groups // X_HI
    top = stored[: top_count * X_HI].reshape(1, X_HI, top_count, col_width)
    send = jnp.broadcast_to(top, (chips, X_HI, top_count, col_width)).reshape(
        chips * X_HI, top_count, col_width
    )
    send = after(send, *steps[1])
    got = lax.all_to_all(send, ("chip", "x_hi"), split_axis=0, concat_axis=0)
    twin = lax.ppermute(got, "core", [(0, 1), (1, 0)])
    core = lax.axis_index("core").astype(jnp.int32).reshape(1)
    upper = order_upper(core, got, twin, y_count)
    upper = after(upper, *steps[2])

    place = jnp.stack([lax.axis_index("x_hi"), lax.axis_index("y")]).astype(jnp.int32)
    offsets, blocks = [0], [panel_lower]
    for distance, step in enumerate(steps, 1):
        offsets += [-distance, distance]
        blocks += step
    far, rest = early_products(place, upper, stored, offsets, blocks)
    far = last_product(place, upper, far, last, True, jnp.bfloat16, 1)
    came = lax.ppermute(far, "x_hi", [(i, X_HI - 1 - i) for i in range(X_HI)])
    rest = last_product(place, upper, rest, last, False, jnp.float32, -1)
    return (rest - came.astype(jnp.float32)).astype(jnp.bfloat16)


def solution(mesh):
    rows, cols = mesh.devices.shape
    split = Mesh(
        mesh.devices.reshape(rows // CORES, CORES, X_HI, cols // X_HI), ("chip", "core", "x_hi", "y")
    )
    col = ("x_hi", "y")
    placed = (P(ROW, col), P(ROW), P(ROW), P(ROW, col))
    return jax.shard_map(
        per_device, mesh=split, in_specs=placed, out_specs=P(ROW, col), check_vma=False
    )
```

```python
import jax
import jax.numpy as jnp
from jax import lax
from jax.experimental import pallas as pl
from jax.experimental.pallas import tpu as pltpu
from jax.sharding import Mesh, PartitionSpec as P

PANEL_W = 4096
X_HI = 2
CORES = 2
PAD = 8
TILE_M = 256
SPLIT = 1024
ROW = ("chip", "core")

inv_root = 0.7071067811865476


def butterfly(top, bottom):
    top = top.astype(jnp.float32)
    bottom = bottom.astype(jnp.float32)
    return jnp.concatenate([(top + bottom) * inv_root, (top - bottom) * inv_root], axis=0)


def after(value, *others):
    return lax.optimization_barrier((value, *others))[0]


VM = pltpu.VMEM


def grant(mib):
    return pltpu.CompilerParams(vmem_limit_bytes=mib << 20)


def whole():
    return pl.BlockSpec(memory_space=VM)


def order_upper(core, got, twin, y_count):
    pairs, top, width = got.shape
    chips = pairs // X_HI
    low = top // y_count
    depth = CORES * chips * low

    def body(core_ref, got_ref, twin_ref, out_ref):
        want = lax.broadcasted_iota(jnp.int32, (depth, depth), 0)
        have = lax.broadcasted_iota(jnp.int32, (depth, depth), 1)
        side = (want % CORES + core_ref[0]) % CORES
        source = side * (chips * low) + want // CORES % chips * low + want // (CORES * chips)
        move = jnp.where(source == have, 1.0, 0.0).astype(got.dtype)
        for y in range(y_count):
            for x in range(X_HI):
                pick = [
                    ref[chip * X_HI + x, y * low : (y + 1) * low] for ref in (got_ref, twin_ref) for chip in range(chips)
                ]
                rows = jnp.dot(move, jnp.concatenate(pick, axis=0), preferred_element_type=jnp.float32)
                out_ref[y, :, x * width : (x + 1) * width] = rows.astype(got.dtype)

    return pl.pallas_call(
        body,
        in_specs=[pl.BlockSpec(memory_space=pltpu.SMEM), whole(), whole()],
        out_specs=whole(),
        out_shape=jax.ShapeDtypeStruct((y_count, depth, X_HI * width), got.dtype),
        compiler_params=grant(8),
        name="order_upper",
    )(core, got, twin)


def early_products(place, upper, stored, offsets, blocks, bounds):
    width = stored.shape[1]
    y_count, depth, both = upper.shape
    flat, where = [], []
    for block in blocks:
        where.append(len(flat))
        flat += block

    def body(place_ref, upper_ref, stored_ref, *refs):
        block_refs, out_refs, turned = refs[: len(flat)], refs[len(flat) : -1], refs[-1]
        for n, offset in enumerate(offsets):
            turned[n * depth : (n + 1) * depth] = upper_ref[(place_ref[1] + offset + y_count) % y_count]
        at_left = place_ref[0] == 0

        for p, (start, stop) in enumerate(bounds):
            far_ref, rest_ref = out_refs[2 * p : 2 * p + 2]

            def one(i, carry):
                local = pl.ds(pl.multiple_of(i * TILE_M, TILE_M), TILE_M)
                full = pl.ds(pl.multiple_of(start + i * TILE_M, TILE_M), TILE_M)
                tiles = [
                    block_refs[n][full] if len(block) == 1 else block_refs[n + p][local]
                    for n, block in zip(where, blocks)
                ]
                total = jnp.dot(jnp.concatenate(tiles, axis=1), turned[...], preferred_element_type=jnp.float32)
                left, right = total[:, :width], total[:, width:]
                far_ref[local] = jnp.where(at_left, right, left)
                rest_ref[local] = stored_ref[full].astype(jnp.float32) - jnp.where(at_left, left, right)
                return carry

            lax.fori_loop(0, (stop - start) // TILE_M, one, 0)

    shapes = [jax.ShapeDtypeStruct((stop - start, width), jnp.float32) for start, stop in bounds for _ in range(2)]
    return pl.pallas_call(
        body,
        in_specs=[pl.BlockSpec(memory_space=pltpu.SMEM)] + [whole()] * (2 + len(flat)),
        out_specs=[whole()] * len(shapes),
        out_shape=shapes,
        scratch_shapes=[VM((len(offsets) * depth, both), upper.dtype)],
        compiler_params=grant(16),
        name="early_products",
    )(place, upper, stored, *flat)


def last_product(place, upper, base, block, partner, out_dtype, sign):
    rows, width = base.shape
    y_count = upper.shape[0]

    def body(place_ref, upper_ref, base_ref, block_ref, out_ref):
        side = (place_ref[0] + 1) % X_HI if partner else place_ref[0]
        columns = upper_ref[(place_ref[1] + y_count // 2) % y_count]
        columns = jnp.where(side == 0, columns[:, :width], columns[:, width:])
        for start in range(0, rows, TILE_M):
            part = slice(start, start + TILE_M)
            term = jnp.dot(block_ref[part], columns, preferred_element_type=jnp.float32)
            out_ref[part] = (base_ref[part] + sign * term).astype(out_ref.dtype)

    return pl.pallas_call(
        body,
        in_specs=[pl.BlockSpec(memory_space=pltpu.SMEM)] + [whole()] * 3,
        out_specs=whole(),
        out_shape=jax.ShapeDtypeStruct((rows, width), out_dtype),
        compiler_params=grant(8),
        name="last_far" if partner else "last_own",
    )(place, upper, base, block)


def per_device(slab_block, scale_first, scale_second, panel_lower):
    row_count, col_width = slab_block.shape
    chips = lax.axis_size("chip")
    groups = chips * CORES
    y_count = lax.axis_size("y")
    block_width = panel_lower.shape[1]
    share = row_count // groups
    half = row_count // 2
    quarter = row_count // 4

    up = [(i, (i + 1) % y_count) for i in range(y_count)]
    down = [(i, (i - 1) % y_count) for i in range(y_count)]
    route = {-1: up, 1: down}
    near = tuple(lax.ppermute(panel_lower, "y", route[sign]) for sign in route)

    first = (scale_first.astype(jnp.float32)[:, None] * slab_block.astype(jnp.float32)).astype(
        jnp.bfloat16
    )
    scale_rows = jnp.pad(
        jnp.transpose(scale_second.reshape(share, groups))[None], ((0, PAD - 1), (0, 0), (0, col_width - share))
    )
    packed = jnp.concatenate([first.reshape(share, groups, col_width), scale_rows], axis=0)
    packed = lax.all_to_all(packed, ROW, split_axis=1, concat_axis=0, tiled=True)
    bounds = ((0, SPLIT), (SPLIT, row_count))
    first_keys, second_keys = ((0, -1), (1, 1)), ((1, -1), (0, 1))
    moving = {}
    for part, sign in first_keys + second_keys:
        start, stop = bounds[part]
        moving[part, sign] = near[0 if sign < 0 else 1][start:stop]
    steps = []
    for distance in range(2, y_count // 2 + 1):
        keys = first_keys if 2 * distance == y_count else first_keys + second_keys
        for part, sign in keys:
            moving[part, sign] = lax.ppermute(moving[part, sign], "y", route[sign])
        steps.append({key: moving[key] for key in keys})
    packed = after(packed, *(steps[0][key] for key in first_keys))
    packed = packed.reshape(groups, share + PAD, col_width)
    cyclic = packed[:, :share].reshape(row_count, col_width)
    scale_cyclic = packed[:, share, :share].reshape(row_count)

    level_one = butterfly(cyclic[:half], cyclic[half:])
    second = (scale_cyclic.astype(jnp.float32)[:, None] * level_one).astype(jnp.bfloat16)
    stored = jnp.concatenate(
        [
            butterfly(second[:quarter], second[quarter:half]),
            butterfly(second[half : half + quarter], second[half + quarter :]),
        ],
        axis=0,
    ).astype(jnp.bfloat16)

    top_count = PANEL_W // groups // X_HI
    top = stored[: top_count * X_HI].reshape(1, X_HI, top_count, col_width)
    send = jnp.broadcast_to(top, (chips, X_HI, top_count, col_width)).reshape(
        chips * X_HI, top_count, col_width
    )
    got = lax.all_to_all(send, ("chip", "x_hi"), split_axis=0, concat_axis=0)
    got = after(got, *steps[1].values())
    twin = lax.ppermute(got, "core", [(0, 1), (1, 0)])
    core = lax.axis_index("core").astype(jnp.int32).reshape(1)
    upper = order_upper(core, got, twin, y_count)
    place = jnp.stack([lax.axis_index("x_hi"), lax.axis_index("y")]).astype(jnp.int32)
    offsets, blocks = [0, -1, 1], [(panel_lower,), near[:1], near[1:]]
    for distance, step in enumerate(steps[:-1], 2):
        for sign in route:
            offsets.append(sign * distance)
            blocks.append((step[0, sign], step[1, sign]))
    sums = early_products(place, upper, stored, offsets, blocks, bounds)
    swap = [(i, X_HI - 1 - i) for i in range(X_HI)]
    out = []
    for key, far, rest in zip(first_keys, sums[::2], sums[1::2]):
        far = last_product(place, upper, far, steps[-1][key], True, jnp.bfloat16, 1)
        came = lax.ppermute(far, "x_hi", swap)
        rest = last_product(place, upper, rest, steps[-1][key], False, jnp.float32, -1)
        out.append((rest - came.astype(jnp.float32)).astype(jnp.bfloat16))
    return jnp.concatenate(out, axis=0)


def solution(mesh):
    rows, cols = mesh.devices.shape
    split = Mesh(
        mesh.devices.reshape(rows // CORES, CORES, X_HI, cols // X_HI), ("chip", "core", "x_hi", "y")
    )
    col = ("x_hi", "y")
    placed = (P(ROW, col), P(ROW), P(ROW), P(ROW, col))
    return jax.shard_map(
        per_device, mesh=split, in_specs=placed, out_specs=P(ROW, col), check_vma=False
    )
```

```python
import jax
import jax.numpy as jnp
from jax import lax
from jax.experimental import pallas as pl
from jax.experimental.pallas import tpu as pltpu
from jax.sharding import Mesh, PartitionSpec as P

PANEL_W = 4096
X_HI = 2
CORES = 2
PAD = 8
TILE_M = 256
GATHERED = 1536
ROW = ("chip", "core")

inv_root = 0.7071067811865476


def butterfly(top, bottom):
    top = top.astype(jnp.float32)
    bottom = bottom.astype(jnp.float32)
    return jnp.concatenate([(top + bottom) * inv_root, (top - bottom) * inv_root], axis=0)


def after(value, *others):
    return lax.optimization_barrier((value, *others))[0]


VM = pltpu.VMEM


def grant(mib):
    return pltpu.CompilerParams(vmem_limit_bytes=mib << 20)


def whole():
    return pl.BlockSpec(memory_space=VM)


def order_upper(core, got, twin, y_count):
    pairs, top, width = got.shape
    chips = pairs // X_HI
    low = top // y_count
    depth = CORES * chips * low

    def body(core_ref, got_ref, twin_ref, out_ref):
        want = lax.broadcasted_iota(jnp.int32, (depth, depth), 0)
        have = lax.broadcasted_iota(jnp.int32, (depth, depth), 1)
        side = (want % CORES + core_ref[0]) % CORES
        source = side * (chips * low) + want // CORES % chips * low + want // (CORES * chips)
        move = jnp.where(source == have, 1.0, 0.0).astype(got.dtype)
        for y in range(y_count):
            for x in range(X_HI):
                pick = [
                    ref[chip * X_HI + x, y * low : (y + 1) * low] for ref in (got_ref, twin_ref) for chip in range(chips)
                ]
                rows = jnp.dot(move, jnp.concatenate(pick, axis=0), preferred_element_type=jnp.float32)
                out_ref[y, :, x * width : (x + 1) * width] = rows.astype(got.dtype)

    return pl.pallas_call(
        body,
        in_specs=[pl.BlockSpec(memory_space=pltpu.SMEM), whole(), whole()],
        out_specs=whole(),
        out_shape=jax.ShapeDtypeStruct((y_count, depth, X_HI * width), got.dtype),
        compiler_params=grant(8),
        name="order_upper",
    )(core, got, twin)


def early_products(place, upper, stored, offsets, blocks, bounds):
    width = stored.shape[1]
    y_count, depth, both = upper.shape
    flat, where = [], []
    for block in blocks:
        where.append(len(flat))
        flat += block

    def body(place_ref, upper_ref, stored_ref, *refs):
        block_refs, out_refs, turned = refs[: len(flat)], refs[len(flat) : -1], refs[-1]
        for n, offset in enumerate(offsets):
            turned[n * depth : (n + 1) * depth] = upper_ref[(place_ref[1] + offset + y_count) % y_count]
        at_left = place_ref[0] == 0

        for p, (start, stop) in enumerate(bounds):
            far_ref, rest_ref = out_refs[2 * p : 2 * p + 2]

            def one(i, carry):
                local = pl.ds(pl.multiple_of(i * TILE_M, TILE_M), TILE_M)
                full = pl.ds(pl.multiple_of(start + i * TILE_M, TILE_M), TILE_M)
                tiles = [
                    block_refs[n][full] if len(block) == 1 else block_refs[n + p][local]
                    for n, block in zip(where, blocks)
                ]
                total = jnp.dot(jnp.concatenate(tiles, axis=1), turned[...], preferred_element_type=jnp.float32)
                left, right = total[:, :width], total[:, width:]
                far_ref[local] = jnp.where(at_left, right, left)
                rest_ref[local] = stored_ref[full].astype(jnp.float32) - jnp.where(at_left, left, right)
                return carry

            lax.fori_loop(0, (stop - start) // TILE_M, one, 0)

    shapes = [jax.ShapeDtypeStruct((stop - start, width), jnp.float32) for start, stop in bounds for _ in range(2)]
    return pl.pallas_call(
        body,
        in_specs=[pl.BlockSpec(memory_space=pltpu.SMEM)] + [whole()] * (2 + len(flat)),
        out_specs=[whole()] * len(shapes),
        out_shape=shapes,
        scratch_shapes=[VM((len(offsets) * depth, both), upper.dtype)],
        compiler_params=grant(16),
        name="early_products",
    )(place, upper, stored, *flat)


def gathered_products(place, upper, stored, lhs):
    rows, depth = lhs.shape
    width = stored.shape[1]
    tile = pl.BlockSpec((TILE_M, width), lambda i, place: (i, 0))
    upper = upper.reshape(depth, upper.shape[2])

    def body(place_ref, upper_ref, stored_ref, lhs_ref, far_ref, rest_ref):
        total = jnp.dot(lhs_ref[...], upper_ref[...], preferred_element_type=jnp.float32)
        left, right = total[:, :width], total[:, width:]
        at_left = place_ref[0] == 0
        far_ref[...] = jnp.where(at_left, right, left).astype(far_ref.dtype)
        rest_ref[...] = stored_ref[...].astype(jnp.float32) - jnp.where(at_left, left, right)

    return pl.pallas_call(
        body,
        grid_spec=pltpu.PrefetchScalarGridSpec(
            num_scalar_prefetch=1,
            grid=(rows // TILE_M,),
            in_specs=[whole(), tile, pl.BlockSpec((TILE_M, depth), lambda i, place: (i, 0))],
            out_specs=[tile, tile],
        ),
        out_shape=[
            jax.ShapeDtypeStruct((rows, width), jnp.bfloat16),
            jax.ShapeDtypeStruct((rows, width), jnp.float32),
        ],
        compiler_params=grant(56),
        name="gathered_products",
    )(place, upper, stored, lhs)


def last_product(place, upper, base, block, partner, out_dtype, sign):
    rows, width = base.shape
    y_count = upper.shape[0]

    def body(place_ref, upper_ref, base_ref, block_ref, out_ref):
        side = (place_ref[0] + 1) % X_HI if partner else place_ref[0]
        columns = upper_ref[(place_ref[1] + y_count // 2) % y_count]
        columns = jnp.where(side == 0, columns[:, :width], columns[:, width:])
        for start in range(0, rows, TILE_M):
            part = slice(start, start + TILE_M)
            term = jnp.dot(block_ref[part], columns, preferred_element_type=jnp.float32)
            out_ref[part] = (base_ref[part] + sign * term).astype(out_ref.dtype)

    return pl.pallas_call(
        body,
        in_specs=[pl.BlockSpec(memory_space=pltpu.SMEM)] + [whole()] * 3,
        out_specs=whole(),
        out_shape=jax.ShapeDtypeStruct((rows, width), out_dtype),
        compiler_params=grant(8),
        name="last_far" if partner else "last_own",
    )(place, upper, base, block)


def per_device(slab_block, scale_first, scale_second, panel_lower):
    row_count, col_width = slab_block.shape
    chips = lax.axis_size("chip")
    groups = chips * CORES
    y_count = lax.axis_size("y")
    block_width = panel_lower.shape[1]
    share = row_count // groups
    half = row_count // 2
    quarter = row_count // 4

    up = [(i, (i + 1) % y_count) for i in range(y_count)]
    down = [(i, (i - 1) % y_count) for i in range(y_count)]
    route = {-1: up, 1: down}
    gathered = lax.all_gather(panel_lower[:GATHERED], "y", axis=1, tiled=True)
    passed = panel_lower[GATHERED:]
    steps, moving = [], (passed, passed)
    for distance in range(1, y_count // 2):
        moving = tuple(lax.ppermute(block, "y", route[sign]) for block, sign in zip(moving, route))
        steps.append(moving)
    middle = passed.shape[0] // 2
    last = (lax.ppermute(moving[0][:middle], "y", up), lax.ppermute(moving[1][middle:], "y", down))

    first = (scale_first.astype(jnp.float32)[:, None] * slab_block.astype(jnp.float32)).astype(
        jnp.bfloat16
    )
    scale_rows = jnp.pad(
        jnp.transpose(scale_second.reshape(share, groups))[None], ((0, PAD - 1), (0, 0), (0, col_width - share))
    )
    packed = jnp.concatenate([first.reshape(share, groups, col_width), scale_rows], axis=0)
    packed = lax.all_to_all(packed, ROW, split_axis=1, concat_axis=0, tiled=True)
    packed = after(packed, *steps[1])
    packed = packed.reshape(groups, share + PAD, col_width)
    cyclic = packed[:, :share].reshape(row_count, col_width)
    scale_cyclic = packed[:, share, :share].reshape(row_count)

    level_one = butterfly(cyclic[:half], cyclic[half:])
    second = (scale_cyclic.astype(jnp.float32)[:, None] * level_one).astype(jnp.bfloat16)
    stored = jnp.concatenate(
        [
            butterfly(second[:quarter], second[quarter:half]),
            butterfly(second[half : half + quarter], second[half + quarter :]),
        ],
        axis=0,
    ).astype(jnp.bfloat16)

    top_count = PANEL_W // groups // X_HI
    top = stored[: top_count * X_HI].reshape(1, X_HI, top_count, col_width)
    send = jnp.broadcast_to(top, (chips, X_HI, top_count, col_width)).reshape(
        chips * X_HI, top_count, col_width
    )
    got = lax.all_to_all(send, ("chip", "x_hi"), split_axis=0, concat_axis=0)
    got = after(got, *steps[2])
    twin = lax.ppermute(got, "core", [(0, 1), (1, 0)])
    core = lax.axis_index("core").astype(jnp.int32).reshape(1)
    upper = order_upper(core, got, twin, y_count)
    place = jnp.stack([lax.axis_index("x_hi"), lax.axis_index("y")]).astype(jnp.int32)
    offsets, blocks = [0], [(passed,)]
    for distance, step in enumerate(steps, 1):
        offsets += [-distance, distance]
        blocks += [(block,) for block in step]
    bounds = ((0, middle), (middle, 2 * middle))
    swap = [(i, X_HI - 1 - i) for i in range(X_HI)]
    sums = early_products(place, upper, stored[GATHERED:], offsets, blocks, bounds)
    fars = [
        last_product(place, upper, far, block, True, jnp.bfloat16, 1) for far, block in zip(sums[::2], last)
    ]
    came_passed = lax.ppermute(jnp.concatenate(fars, axis=0), "x_hi", swap)
    rests = [
        last_product(place, upper, rest, block, False, jnp.float32, -1) for rest, block in zip(sums[1::2], last)
    ]
    upper, _ = lax.optimization_barrier((upper, came_passed))
    far, rest = gathered_products(place, upper, stored[:GATHERED], gathered)
    came = lax.ppermute(far, "x_hi", swap)
    rest = jnp.concatenate([rest, *rests], axis=0)
    came = jnp.concatenate([came, came_passed], axis=0)
    return (rest - came.astype(jnp.float32)).astype(jnp.bfloat16)


def solution(mesh):
    rows, cols = mesh.devices.shape
    split = Mesh(
        mesh.devices.reshape(rows // CORES, CORES, X_HI, cols // X_HI), ("chip", "core", "x_hi", "y")
    )
    col = ("x_hi", "y")
    placed = (P(ROW, col), P(ROW), P(ROW), P(ROW, col))
    return jax.shard_map(
        per_device, mesh=split, in_specs=placed, out_specs=P(ROW, col), check_vma=False
    )
```

```python
import jax
import jax.numpy as jnp
from jax import lax
from jax.experimental import pallas as pl
from jax.experimental.pallas import tpu as pltpu
from jax.sharding import Mesh, PartitionSpec as P

PANEL_W = 4096
X_HI = 2
CORES = 2
PAD = 8
TILE_M = 256
PARTS = 2
ROW = ("chip", "core")

inv_root = 0.7071067811865476


def butterfly(top, bottom):
    top = top.astype(jnp.float32)
    bottom = bottom.astype(jnp.float32)
    return jnp.concatenate([(top + bottom) * inv_root, (top - bottom) * inv_root], axis=0)


def after(value, *others):
    return lax.optimization_barrier((value, *others))[0]


VM = pltpu.VMEM


def grant(mib):
    return pltpu.CompilerParams(vmem_limit_bytes=mib << 20)


def whole():
    return pl.BlockSpec(memory_space=VM)


def order_upper(core, got, twin, y_count):
    pairs, top, width = got.shape
    chips = pairs // X_HI
    low = top // y_count
    depth = CORES * chips * low

    def body(core_ref, got_ref, twin_ref, out_ref):
        want = lax.broadcasted_iota(jnp.int32, (depth, depth), 0)
        have = lax.broadcasted_iota(jnp.int32, (depth, depth), 1)
        side = (want % CORES + core_ref[0]) % CORES
        source = side * (chips * low) + want // CORES % chips * low + want // (CORES * chips)
        move = jnp.where(source == have, 1.0, 0.0).astype(got.dtype)
        for y in range(y_count):
            for x in range(X_HI):
                pick = [
                    ref[chip * X_HI + x, y * low : (y + 1) * low] for ref in (got_ref, twin_ref) for chip in range(chips)
                ]
                rows = jnp.dot(move, jnp.concatenate(pick, axis=0), preferred_element_type=jnp.float32)
                out_ref[y, :, x * width : (x + 1) * width] = rows.astype(got.dtype)

    return pl.pallas_call(
        body,
        in_specs=[pl.BlockSpec(memory_space=pltpu.SMEM), whole(), whole()],
        out_specs=whole(),
        out_shape=jax.ShapeDtypeStruct((y_count, depth, X_HI * width), got.dtype),
        compiler_params=grant(8),
        name="order_upper",
    )(core, got, twin)


def early_products(place, upper, stored, offsets, blocks, start, rows):
    width = stored.shape[1]
    y_count, depth, both = upper.shape
    bases = [start if block.shape[0] > rows else 0 for block in blocks]

    def body(place_ref, upper_ref, stored_ref, *refs):
        *block_refs, far_ref, rest_ref, turned = refs
        for n, offset in enumerate(offsets):
            turned[n * depth : (n + 1) * depth] = upper_ref[(place_ref[1] + offset + y_count) % y_count]
        at_left = place_ref[0] == 0

        def one(i, carry):
            tile = lambda base: pl.ds(pl.multiple_of(base + i * TILE_M, TILE_M), TILE_M)
            lhs = jnp.concatenate([ref[tile(base)] for ref, base in zip(block_refs, bases)], axis=1)
            total = jnp.dot(lhs, turned[...], preferred_element_type=jnp.float32)
            left, right = total[:, :width], total[:, width:]
            far_ref[tile(0)] = jnp.where(at_left, right, left)
            rest_ref[tile(0)] = stored_ref[tile(start)].astype(jnp.float32) - jnp.where(at_left, left, right)
            return carry

        lax.fori_loop(0, rows // TILE_M, one, 0)

    return pl.pallas_call(
        body,
        in_specs=[pl.BlockSpec(memory_space=pltpu.SMEM)] + [whole()] * (2 + len(blocks)),
        out_specs=[whole(), whole()],
        out_shape=[jax.ShapeDtypeStruct((rows, width), jnp.float32)] * 2,
        scratch_shapes=[VM((len(offsets) * depth, both), upper.dtype)],
        compiler_params=grant(8),
        name="early_products",
    )(place, upper, stored, *blocks)


def last_product(place, upper, base, halves, partner, out_dtype, sign):
    rows, width = base.shape
    y_count = upper.shape[0]
    half = rows // len(halves)
    step = min(half, TILE_M)

    def body(place_ref, upper_ref, base_ref, *refs):
        *half_refs, out_ref = refs
        side = (place_ref[0] + 1) % X_HI if partner else place_ref[0]
        columns = upper_ref[(place_ref[1] + y_count // 2) % y_count]
        columns = jnp.where(side == 0, columns[:, :width], columns[:, width:])
        for n, ref in enumerate(half_refs):
            for start in range(0, half, step):
                part = slice(n * half + start, n * half + start + step)
                term = jnp.dot(ref[start : start + step], columns, preferred_element_type=jnp.float32)
                out_ref[part] = (base_ref[part] + sign * term).astype(out_ref.dtype)

    return pl.pallas_call(
        body,
        in_specs=[pl.BlockSpec(memory_space=pltpu.SMEM)] + [whole()] * (2 + len(halves)),
        out_specs=whole(),
        out_shape=jax.ShapeDtypeStruct((rows, width), out_dtype),
        compiler_params=grant(8),
        name="last_far" if partner else "last_own",
    )(place, upper, base, *halves)


def per_device(slab_block, scale_first, scale_second, panel_lower):
    row_count, col_width = slab_block.shape
    chips = lax.axis_size("chip")
    groups = chips * CORES
    y_count = lax.axis_size("y")
    block_width = panel_lower.shape[1]
    share = row_count // groups
    half = row_count // 2
    quarter = row_count // 4
    part_rows = row_count // PARTS

    up = [(i, (i + 1) % y_count) for i in range(y_count)]
    down = [(i, (i - 1) % y_count) for i in range(y_count)]
    route = {-1: up, 1: down}
    near = tuple(lax.ppermute(panel_lower, "y", route[sign]) for sign in route)

    first = (scale_first.astype(jnp.float32)[:, None] * slab_block.astype(jnp.float32)).astype(
        jnp.bfloat16
    )
    scale_rows = jnp.pad(
        jnp.transpose(scale_second.reshape(share, groups))[None], ((0, PAD - 1), (0, 0), (0, col_width - share))
    )
    packed = jnp.concatenate([first.reshape(share, groups, col_width), scale_rows], axis=0)
    packed = lax.all_to_all(packed, ROW, split_axis=1, concat_axis=0, tiled=True)
    joined = jnp.concatenate(near, axis=1)
    packed = after(packed, joined)
    far_near = tuple(lax.ppermute(block, "y", route[sign]) for block, sign in zip(near, route))
    third, last = [], []
    for part in range(PARTS):
        rows = slice(part * part_rows, (part + 1) * part_rows)
        pair = tuple(lax.ppermute(block[rows], "y", route[sign]) for block, sign in zip(far_near, route))
        middle = part_rows // 2
        third.append(pair)
        last.append((lax.ppermute(pair[0][:middle], "y", up), lax.ppermute(pair[1][middle:], "y", down)))
    packed = packed.reshape(groups, share + PAD, col_width)
    cyclic = packed[:, :share].reshape(row_count, col_width)
    scale_cyclic = packed[:, share, :share].reshape(row_count)

    level_one = butterfly(cyclic[:half], cyclic[half:])
    second = (scale_cyclic.astype(jnp.float32)[:, None] * level_one).astype(jnp.bfloat16)
    stored = jnp.concatenate(
        [
            butterfly(second[:quarter], second[quarter:half]),
            butterfly(second[half : half + quarter], second[half + quarter :]),
        ],
        axis=0,
    ).astype(jnp.bfloat16)

    top_count = PANEL_W // groups // X_HI
    top = stored[: top_count * X_HI].reshape(1, X_HI, top_count, col_width)
    send = jnp.broadcast_to(top, (chips, X_HI, top_count, col_width)).reshape(
        chips * X_HI, top_count, col_width
    )
    got = lax.all_to_all(send, ("chip", "x_hi"), split_axis=0, concat_axis=0)
    got = after(got, *third[0])
    twin = lax.ppermute(got, "core", [(0, 1), (1, 0)])
    core = lax.axis_index("core").astype(jnp.int32).reshape(1)
    upper = order_upper(core, got, twin, y_count)
    place = jnp.stack([lax.axis_index("x_hi"), lax.axis_index("y")]).astype(jnp.int32)
    offsets = [0, -1, 1, -2, 2, -3, 3]
    swap = [(i, X_HI - 1 - i) for i in range(X_HI)]
    out = []
    for part in range(PARTS):
        blocks = [panel_lower, joined, *far_near, *third[part]]
        far, rest = early_products(place, upper, stored, offsets, blocks, part * part_rows, part_rows)
        far = last_product(place, upper, far, last[part], True, jnp.bfloat16, 1)
        upper = after(upper, far)
        came = lax.ppermute(far, "x_hi", swap)
        rest = last_product(place, upper, rest, last[part], False, jnp.float32, -1)
        out.append((rest - came.astype(jnp.float32)).astype(jnp.bfloat16))
    return jnp.concatenate(out, axis=0)


def solution(mesh):
    rows, cols = mesh.devices.shape
    split = Mesh(
        mesh.devices.reshape(rows // CORES, CORES, X_HI, cols // X_HI), ("chip", "core", "x_hi", "y")
    )
    col = ("x_hi", "y")
    placed = (P(ROW, col), P(ROW), P(ROW), P(ROW, col))
    return jax.shard_map(
        per_device, mesh=split, in_specs=placed, out_specs=P(ROW, col), check_vma=False
    )
```

```python
import jax
import jax.numpy as jnp
from jax import lax
from jax.experimental import pallas as pl
from jax.experimental.pallas import tpu as pltpu
from jax.sharding import Mesh, PartitionSpec as P

PANEL_W = 4096
X_HI = 2
CORES = 2
PAD = 8
TILE_M = 256
ROW = ("chip", "core")

inv_root = 0.7071067811865476


def butterfly(top, bottom):
    top = top.astype(jnp.float32)
    bottom = bottom.astype(jnp.float32)
    return jnp.concatenate([(top + bottom) * inv_root, (top - bottom) * inv_root], axis=0)


def after(value, *others):
    return lax.optimization_barrier((value, *others))[0]


VM = pltpu.VMEM


def grant(mib):
    return pltpu.CompilerParams(vmem_limit_bytes=mib << 20)


def whole():
    return pl.BlockSpec(memory_space=VM)


def order_upper(core, got, twin, y_count):
    pairs, top, width = got.shape
    chips = pairs // X_HI
    low = top // y_count
    depth = CORES * chips * low

    def body(core_ref, got_ref, twin_ref, out_ref):
        want = lax.broadcasted_iota(jnp.int32, (depth, depth), 0)
        have = lax.broadcasted_iota(jnp.int32, (depth, depth), 1)
        side = (want % CORES + core_ref[0]) % CORES
        source = side * (chips * low) + want // CORES % chips * low + want // (CORES * chips)
        move = jnp.where(source == have, 1.0, 0.0).astype(got.dtype)
        for y in range(y_count):
            for x in range(X_HI):
                pick = [
                    ref[chip * X_HI + x, y * low : (y + 1) * low] for ref in (got_ref, twin_ref) for chip in range(chips)
                ]
                rows = jnp.dot(move, jnp.concatenate(pick, axis=0), preferred_element_type=jnp.float32)
                out_ref[y, :, x * width : (x + 1) * width] = rows.astype(got.dtype)

    return pl.pallas_call(
        body,
        in_specs=[pl.BlockSpec(memory_space=pltpu.SMEM), whole(), whole()],
        out_specs=whole(),
        out_shape=jax.ShapeDtypeStruct((y_count, depth, X_HI * width), got.dtype),
        compiler_params=grant(8),
        name="order_upper",
    )(core, got, twin)


def early_products(place, upper, stored, offsets, blocks):
    rows, width = stored.shape
    y_count, depth, both = upper.shape
    flat, where = [], []
    for block in blocks:
        where.append(len(flat))
        flat += block

    def body(place_ref, upper_ref, stored_ref, *refs):
        block_refs, (far_ref, rest_ref, turned) = refs[: len(flat)], refs[len(flat) :]
        for n, offset in enumerate(offsets):
            turned[n * depth : (n + 1) * depth] = upper_ref[(place_ref[1] + offset + y_count) % y_count]
        at_left = place_ref[0] == 0

        for part in range(2):

            def one(i, carry):
                local = pl.ds(pl.multiple_of(i * TILE_M, TILE_M), TILE_M)
                full = pl.ds(pl.multiple_of(part * (rows // 2) + i * TILE_M, TILE_M), TILE_M)
                tiles = [
                    block_refs[n][full] if len(block) == 1 else block_refs[n + part][local]
                    for n, block in zip(where, blocks)
                ]
                total = jnp.dot(jnp.concatenate(tiles, axis=1), turned[...], preferred_element_type=jnp.float32)
                left, right = total[:, :width], total[:, width:]
                far_ref[full] = jnp.where(at_left, right, left)
                rest_ref[full] = stored_ref[full].astype(jnp.float32) - jnp.where(at_left, left, right)
                return carry

            lax.fori_loop(0, rows // 2 // TILE_M, one, 0)

    return pl.pallas_call(
        body,
        in_specs=[pl.BlockSpec(memory_space=pltpu.SMEM)] + [whole()] * (2 + len(flat)),
        out_specs=[whole(), whole()],
        out_shape=[jax.ShapeDtypeStruct((rows, width), jnp.float32)] * 2,
        scratch_shapes=[VM((len(offsets) * depth, both), upper.dtype)],
        compiler_params=grant(16),
        name="early_products",
    )(place, upper, stored, *flat)


def last_product(place, upper, base, halves, partner, out_dtype, sign):
    rows, width = base.shape
    y_count = upper.shape[0]
    half = rows // len(halves)
    step = min(half, TILE_M)

    def body(place_ref, upper_ref, base_ref, *refs):
        *half_refs, out_ref = refs
        side = (place_ref[0] + 1) % X_HI if partner else place_ref[0]
        columns = upper_ref[(place_ref[1] + y_count // 2) % y_count]
        columns = jnp.where(side == 0, columns[:, :width], columns[:, width:])
        for n, ref in enumerate(half_refs):
            for start in range(0, half, step):
                part = slice(n * half + start, n * half + start + step)
                term = jnp.dot(ref[start : start + step], columns, preferred_element_type=jnp.float32)
                out_ref[part] = (base_ref[part] + sign * term).astype(out_ref.dtype)

    return pl.pallas_call(
        body,
        in_specs=[pl.BlockSpec(memory_space=pltpu.SMEM)] + [whole()] * (2 + len(halves)),
        out_specs=whole(),
        out_shape=jax.ShapeDtypeStruct((rows, width), out_dtype),
        compiler_params=grant(8),
        name="last_far" if partner else "last_own",
    )(place, upper, base, *halves)


def per_device(slab_block, scale_first, scale_second, panel_lower):
    row_count, col_width = slab_block.shape
    chips = lax.axis_size("chip")
    groups = chips * CORES
    y_count = lax.axis_size("y")
    block_width = panel_lower.shape[1]
    share = row_count // groups
    half = row_count // 2
    quarter = row_count // 4

    up = [(i, (i + 1) % y_count) for i in range(y_count)]
    down = [(i, (i - 1) % y_count) for i in range(y_count)]
    route = {-1: up, 1: down}
    near = tuple(lax.ppermute(panel_lower, "y", route[sign]) for sign in route)

    first = (scale_first.astype(jnp.float32)[:, None] * slab_block.astype(jnp.float32)).astype(
        jnp.bfloat16
    )
    scale_rows = jnp.pad(
        jnp.transpose(scale_second.reshape(share, groups))[None], ((0, PAD - 1), (0, 0), (0, col_width - share))
    )
    packed = jnp.concatenate([first.reshape(share, groups, col_width), scale_rows], axis=0)
    packed = lax.all_to_all(packed, ROW, split_axis=1, concat_axis=0, tiled=True)
    joined = jnp.concatenate(near, axis=1)
    packed = after(packed, joined)
    far_near = tuple(lax.ppermute(block, "y", route[sign]) for block, sign in zip(near, route))
    first_keys, second_keys = ((0, -1), (1, 1)), ((1, -1), (0, 1))
    third = {}
    for part, sign in first_keys + second_keys:
        block = far_near[0 if sign < 0 else 1][part * half : (part + 1) * half]
        third[part, sign] = lax.ppermute(block, "y", route[sign])
    last = [lax.ppermute(third[part, sign], "y", route[sign]) for part, sign in first_keys]
    packed = packed.reshape(groups, share + PAD, col_width)
    cyclic = packed[:, :share].reshape(row_count, col_width)
    scale_cyclic = packed[:, share, :share].reshape(row_count)

    level_one = butterfly(cyclic[:half], cyclic[half:])
    second = (scale_cyclic.astype(jnp.float32)[:, None] * level_one).astype(jnp.bfloat16)
    stored = jnp.concatenate(
        [
            butterfly(second[:quarter], second[quarter:half]),
            butterfly(second[half : half + quarter], second[half + quarter :]),
        ],
        axis=0,
    ).astype(jnp.bfloat16)

    top_count = PANEL_W // groups // X_HI
    top = stored[: top_count * X_HI].reshape(1, X_HI, top_count, col_width)
    send = jnp.broadcast_to(top, (chips, X_HI, top_count, col_width)).reshape(
        chips * X_HI, top_count, col_width
    )
    got = lax.all_to_all(send, ("chip", "x_hi"), split_axis=0, concat_axis=0)
    got = after(got, *(third[key] for key in first_keys))
    twin = lax.ppermute(got, "core", [(0, 1), (1, 0)])
    twin = after(twin, *(third[key] for key in second_keys))
    core = lax.axis_index("core").astype(jnp.int32).reshape(1)
    upper = order_upper(core, got, twin, y_count)
    place = jnp.stack([lax.axis_index("x_hi"), lax.axis_index("y")]).astype(jnp.int32)
    offsets = [0, -1, 1, -2, 2, -3, 3]
    blocks = [(panel_lower,), (joined,), far_near[:1], far_near[1:]]
    blocks += [(third[0, sign], third[1, sign]) for sign in route]
    far, rest = early_products(place, upper, stored, offsets, blocks)
    far = last_product(place, upper, far, last, True, jnp.bfloat16, 1)
    came = lax.ppermute(far, "x_hi", [(i, X_HI - 1 - i) for i in range(X_HI)])
    rest = last_product(place, upper, rest, last, False, jnp.float32, -1)
    return (rest - came.astype(jnp.float32)).astype(jnp.bfloat16)


def solution(mesh):
    rows, cols = mesh.devices.shape
    split = Mesh(
        mesh.devices.reshape(rows // CORES, CORES, X_HI, cols // X_HI), ("chip", "core", "x_hi", "y")
    )
    col = ("x_hi", "y")
    placed = (P(ROW, col), P(ROW), P(ROW), P(ROW, col))
    return jax.shard_map(
        per_device, mesh=split, in_specs=placed, out_specs=P(ROW, col), check_vma=False
    )
```

```python
import jax
import jax.numpy as jnp
from jax import lax
from jax.experimental import pallas as pl
from jax.experimental.pallas import tpu as pltpu
from jax.sharding import Mesh, PartitionSpec as P

PANEL_W = 4096
X_HI = 2
CORES = 2
PAD = 8
TILE_M = 256
ROW = ("chip", "core")

inv_root = 0.7071067811865476


def butterfly(top, bottom):
    top = top.astype(jnp.float32)
    bottom = bottom.astype(jnp.float32)
    return jnp.concatenate([(top + bottom) * inv_root, (top - bottom) * inv_root], axis=0)


def after(value, *others):
    return lax.optimization_barrier((value, *others))[0]


VM = pltpu.VMEM


def grant(mib):
    return pltpu.CompilerParams(vmem_limit_bytes=mib << 20)


def whole():
    return pl.BlockSpec(memory_space=VM)


def order_upper(core, got, twin, y_count):
    pairs, top, width = got.shape
    chips = pairs // X_HI
    low = top // y_count
    depth = CORES * chips * low

    def body(core_ref, got_ref, twin_ref, out_ref):
        want = lax.broadcasted_iota(jnp.int32, (depth, depth), 0)
        have = lax.broadcasted_iota(jnp.int32, (depth, depth), 1)
        side = (want % CORES + core_ref[0]) % CORES
        source = side * (chips * low) + want // CORES % chips * low + want // (CORES * chips)
        move = jnp.where(source == have, 1.0, 0.0).astype(got.dtype)
        for y in range(y_count):
            for x in range(X_HI):
                pick = [
                    ref[chip * X_HI + x, y * low : (y + 1) * low] for ref in (got_ref, twin_ref) for chip in range(chips)
                ]
                rows = jnp.dot(move, jnp.concatenate(pick, axis=0), preferred_element_type=jnp.float32)
                out_ref[y, :, x * width : (x + 1) * width] = rows.astype(got.dtype)

    return pl.pallas_call(
        body,
        in_specs=[pl.BlockSpec(memory_space=pltpu.SMEM), whole(), whole()],
        out_specs=whole(),
        out_shape=jax.ShapeDtypeStruct((y_count, depth, X_HI * width), got.dtype),
        compiler_params=grant(8),
        name="order_upper",
    )(core, got, twin)


def early_products(place, upper, stored, offsets, blocks, own_offsets, own_blocks):
    rows, width = stored.shape
    y_count, depth, both = upper.shape
    parts = len(own_blocks)
    share = rows // parts
    common = len(offsets) * depth

    def body(place_ref, upper_ref, stored_ref, *refs):
        block_refs, own_refs, out_refs = refs[: len(blocks)], refs[len(blocks) : -1 - 2 * parts], refs[-1 - 2 * parts : -1]
        turned = refs[-1]
        for n, offset in enumerate(offsets):
            turned[n * depth : (n + 1) * depth] = upper_ref[(place_ref[1] + offset + y_count) % y_count]
        at_left = place_ref[0] == 0

        for part in range(parts):
            turned[common:] = upper_ref[(place_ref[1] + own_offsets[part] + y_count) % y_count]
            far_ref, rest_ref = out_refs[2 * part : 2 * part + 2]

            def one(i, carry):
                local = pl.ds(pl.multiple_of(i * TILE_M, TILE_M), TILE_M)
                full = pl.ds(pl.multiple_of(part * share + i * TILE_M, TILE_M), TILE_M)
                tiles = [ref[full] for ref in block_refs] + [own_refs[part][local]]
                total = jnp.dot(jnp.concatenate(tiles, axis=1), turned[...], preferred_element_type=jnp.float32)
                left, right = total[:, :width], total[:, width:]
                far_ref[local] = jnp.where(at_left, right, left)
                rest_ref[local] = stored_ref[full].astype(jnp.float32) - jnp.where(at_left, left, right)
                return carry

            lax.fori_loop(0, share // TILE_M, one, 0)

    return pl.pallas_call(
        body,
        in_specs=[pl.BlockSpec(memory_space=pltpu.SMEM)] + [whole()] * (2 + len(blocks) + parts),
        out_specs=[whole()] * (2 * parts),
        out_shape=[jax.ShapeDtypeStruct((share, width), jnp.float32)] * (2 * parts),
        scratch_shapes=[VM((common + depth, both), upper.dtype)],
        compiler_params=grant(16),
        name="early_products",
    )(place, upper, stored, *blocks, *own_blocks)


def last_product(place, upper, base, offsets, blocks, partner, out_dtype, sign):
    rows, width = base.shape
    y_count = upper.shape[0]

    def body(place_ref, upper_ref, base_ref, *refs):
        *block_refs, out_ref = refs
        side = (place_ref[0] + 1) % X_HI if partner else place_ref[0]
        columns = []
        for offset in offsets:
            both = upper_ref[(place_ref[1] + offset + y_count) % y_count]
            columns.append(jnp.where(side == 0, both[:, :width], both[:, width:]))
        columns = jnp.concatenate(columns, axis=0)
        for start in range(0, rows, TILE_M):
            part = slice(start, start + TILE_M)
            lhs = jnp.concatenate([ref[part] for ref in block_refs], axis=1)
            term = jnp.dot(lhs, columns, preferred_element_type=jnp.float32)
            out_ref[part] = (base_ref[part] + sign * term).astype(out_ref.dtype)

    return pl.pallas_call(
        body,
        in_specs=[pl.BlockSpec(memory_space=pltpu.SMEM)] + [whole()] * (2 + len(blocks)),
        out_specs=whole(),
        out_shape=jax.ShapeDtypeStruct((rows, width), out_dtype),
        compiler_params=grant(8),
        name="last_far" if partner else "last_own",
    )(place, upper, base, *blocks)


def per_device(slab_block, scale_first, scale_second, panel_lower):
    row_count, col_width = slab_block.shape
    chips = lax.axis_size("chip")
    groups = chips * CORES
    y_count = lax.axis_size("y")
    block_width = panel_lower.shape[1]
    share = row_count // groups
    half = row_count // 2
    quarter = row_count // 4

    up = [(i, (i + 1) % y_count) for i in range(y_count)]
    down = [(i, (i - 1) % y_count) for i in range(y_count)]
    route = {-1: up, 1: down}
    near = tuple(lax.ppermute(panel_lower, "y", route[sign]) for sign in route)

    first = (scale_first.astype(jnp.float32)[:, None] * slab_block.astype(jnp.float32)).astype(
        jnp.bfloat16
    )
    scale_rows = jnp.pad(
        jnp.transpose(scale_second.reshape(share, groups))[None], ((0, PAD - 1), (0, 0), (0, col_width - share))
    )
    packed = jnp.concatenate([first.reshape(share, groups, col_width), scale_rows], axis=0)
    packed = lax.all_to_all(packed, ROW, split_axis=1, concat_axis=0, tiled=True)
    joined = jnp.concatenate(near, axis=1)
    packed = after(packed, joined)
    far_near = tuple(lax.ppermute(block, "y", route[sign]) for block, sign in zip(near, route))
    first_keys, second_keys = ((0, -1), (1, 1)), ((1, -1), (0, 1))
    third = {}
    for part, sign in first_keys + second_keys:
        block = far_near[0 if sign < 0 else 1][part * half : (part + 1) * half]
        third[part, sign] = lax.ppermute(block, "y", route[sign])
    last = [lax.ppermute(third[part, sign], "y", route[sign]) for part, sign in first_keys]
    packed = packed.reshape(groups, share + PAD, col_width)
    cyclic = packed[:, :share].reshape(row_count, col_width)
    scale_cyclic = packed[:, share, :share].reshape(row_count)

    level_one = butterfly(cyclic[:half], cyclic[half:])
    second = (scale_cyclic.astype(jnp.float32)[:, None] * level_one).astype(jnp.bfloat16)
    stored = jnp.concatenate(
        [
            butterfly(second[:quarter], second[quarter:half]),
            butterfly(second[half : half + quarter], second[half + quarter :]),
        ],
        axis=0,
    ).astype(jnp.bfloat16)

    top_count = PANEL_W // groups // X_HI
    top = stored[: top_count * X_HI].reshape(1, X_HI, top_count, col_width)
    send = jnp.broadcast_to(top, (chips, X_HI, top_count, col_width)).reshape(
        chips * X_HI, top_count, col_width
    )
    got = lax.all_to_all(send, ("chip", "x_hi"), split_axis=0, concat_axis=0)
    got = after(got, third[0, -1])
    twin = lax.ppermute(got, "core", [(0, 1), (1, 0)])
    twin = after(twin, *(third[key] for key in second_keys))
    core = lax.axis_index("core").astype(jnp.int32).reshape(1)
    upper = order_upper(core, got, twin, y_count)
    place = jnp.stack([lax.axis_index("x_hi"), lax.axis_index("y")]).astype(jnp.int32)
    swap = [(i, X_HI - 1 - i) for i in range(X_HI)]
    sums = early_products(
        place,
        upper,
        stored,
        [0, -1, 1, -2, 2],
        [panel_lower, joined, *far_near],
        [sign * (y_count // 2 - 1) for _, sign in first_keys],
        [third[key] for key in first_keys],
    )
    out = []
    for part, sign in first_keys:
        offsets = [-sign * (y_count // 2 - 1), y_count // 2]
        blocks = [third[part, -sign], last[part]]
        far = last_product(place, upper, sums[2 * part], offsets, blocks, True, jnp.bfloat16, 1)
        came = lax.ppermute(far, "x_hi", swap)
        rest = last_product(place, upper, sums[2 * part + 1], offsets, blocks, False, jnp.float32, -1)
        out.append((rest - came.astype(jnp.float32)).astype(jnp.bfloat16))
    return jnp.concatenate(out, axis=0)


def solution(mesh):
    rows, cols = mesh.devices.shape
    split = Mesh(
        mesh.devices.reshape(rows // CORES, CORES, X_HI, cols // X_HI), ("chip", "core", "x_hi", "y")
    )
    col = ("x_hi", "y")
    placed = (P(ROW, col), P(ROW), P(ROW), P(ROW, col))
    return jax.shard_map(
        per_device, mesh=split, in_specs=placed, out_specs=P(ROW, col), check_vma=False
    )
```

```python
import jax
import jax.numpy as jnp
from jax import lax
from jax.experimental import pallas as pl
from jax.experimental.pallas import tpu as pltpu
from jax.sharding import Mesh, PartitionSpec as P

PANEL_W = 4096
X_HI = 2
CORES = 2
PAD = 8
TILE_M = 256
SPLIT = 1024
ROW = ("chip", "core")

inv_root = 0.7071067811865476


def butterfly(top, bottom):
    top = top.astype(jnp.float32)
    bottom = bottom.astype(jnp.float32)
    return jnp.concatenate([(top + bottom) * inv_root, (top - bottom) * inv_root], axis=0)


def after(value, *others):
    return lax.optimization_barrier((value, *others))[0]


VM = pltpu.VMEM


def grant(mib):
    return pltpu.CompilerParams(vmem_limit_bytes=mib << 20)


def whole():
    return pl.BlockSpec(memory_space=VM)


def order_upper(core, got_ref, twin_ref, out_ref):
    pairs, top, width = got_ref.shape
    y_count, depth = out_ref.shape[:2]
    chips, low = pairs // X_HI, top // y_count
    want = lax.broadcasted_iota(jnp.int32, (depth, depth), 0)
    have = lax.broadcasted_iota(jnp.int32, (depth, depth), 1)
    side = (want % CORES + core) % CORES
    source = side * (chips * low) + want // CORES % chips * low + want // (CORES * chips)
    move = jnp.where(source == have, 1.0, 0.0).astype(out_ref.dtype)
    for y in range(y_count):
        for x in range(X_HI):
            pick = [ref[chip * X_HI + x, y * low : (y + 1) * low] for ref in (got_ref, twin_ref) for chip in range(chips)]
            rows = jnp.dot(move, jnp.concatenate(pick, axis=0), preferred_element_type=jnp.float32)
            out_ref[y, :, x * width : (x + 1) * width] = rows.astype(out_ref.dtype)


def early_products(place, got, twin, stored, bounds, offsets, blocks, own_offsets, own_blocks):
    rows, width = stored.shape
    y_count = lax.axis_size("y")
    depth, both = blocks[0].shape[1], X_HI * width
    parts = len(own_blocks)
    common = len(offsets) * depth

    def body(place_ref, got_ref, twin_ref, stored_ref, *refs):
        block_refs, own_refs, out_refs = refs[: len(blocks)], refs[len(blocks) : -2 - 2 * parts], refs[-2 - 2 * parts : -2]
        upper_ref, turned = refs[-2:]
        order_upper(place_ref[2], got_ref, twin_ref, upper_ref)
        for n, offset in enumerate(offsets):
            turned[n * depth : (n + 1) * depth] = upper_ref[(place_ref[1] + offset + y_count) % y_count]
        at_left = place_ref[0] == 0

        for part, (start, stop) in enumerate(bounds):
            turned[common:] = upper_ref[(place_ref[1] + own_offsets[part] + y_count) % y_count]
            far_ref, rest_ref = out_refs[2 * part : 2 * part + 2]

            def one(i, carry):
                local = pl.ds(pl.multiple_of(i * TILE_M, TILE_M), TILE_M)
                full = pl.ds(pl.multiple_of(start + i * TILE_M, TILE_M), TILE_M)
                tiles = [ref[full] for ref in block_refs] + [own_refs[part][local]]
                total = jnp.dot(jnp.concatenate(tiles, axis=1), turned[...], preferred_element_type=jnp.float32)
                left, right = total[:, :width], total[:, width:]
                far_ref[local] = jnp.where(at_left, right, left)
                rest_ref[local] = stored_ref[full].astype(jnp.float32) - jnp.where(at_left, left, right)
                return carry

            lax.fori_loop(0, (stop - start) // TILE_M, one, 0)

    return pl.pallas_call(
        body,
        in_specs=[pl.BlockSpec(memory_space=pltpu.SMEM)] + [whole()] * (3 + len(blocks) + parts),
        out_specs=[whole()] * (2 * parts + 1),
        out_shape=[jax.ShapeDtypeStruct((b - a, width), jnp.float32) for a, b in bounds for _ in range(2)]
        + [jax.ShapeDtypeStruct((y_count, depth, both), stored.dtype)],
        scratch_shapes=[VM((common + depth, both), stored.dtype)],
        compiler_params=grant(16),
        name="early_products",
    )(place, got, twin, stored, *blocks, *own_blocks)


def last_product(place, upper, base, offsets, blocks, partner, out_dtype, sign):
    rows, width = base.shape
    y_count = upper.shape[0]

    def body(place_ref, upper_ref, base_ref, *refs):
        *block_refs, out_ref = refs
        side = (place_ref[0] + 1) % X_HI if partner else place_ref[0]
        columns = []
        for offset in offsets:
            both = upper_ref[(place_ref[1] + offset + y_count) % y_count]
            columns.append(jnp.where(side == 0, both[:, :width], both[:, width:]))
        columns = jnp.concatenate(columns, axis=0)
        for start in range(0, rows, TILE_M):
            part = slice(start, start + TILE_M)
            lhs = jnp.concatenate([ref[part] for ref in block_refs], axis=1)
            term = jnp.dot(lhs, columns, preferred_element_type=jnp.float32)
            out_ref[part] = (base_ref[part] + sign * term).astype(out_ref.dtype)

    return pl.pallas_call(
        body,
        in_specs=[pl.BlockSpec(memory_space=pltpu.SMEM)] + [whole()] * (2 + len(blocks)),
        out_specs=whole(),
        out_shape=jax.ShapeDtypeStruct((rows, width), out_dtype),
        compiler_params=grant(8),
        name="last_far" if partner else "last_own",
    )(place, upper, base, *blocks)


def per_device(slab_block, scale_first, scale_second, panel_lower):
    row_count, col_width = slab_block.shape
    chips = lax.axis_size("chip")
    groups = chips * CORES
    y_count = lax.axis_size("y")
    block_width = panel_lower.shape[1]
    share = row_count // groups
    half = row_count // 2
    quarter = row_count // 4

    up = [(i, (i + 1) % y_count) for i in range(y_count)]
    down = [(i, (i - 1) % y_count) for i in range(y_count)]
    route = {-1: up, 1: down}
    near = tuple(lax.ppermute(panel_lower, "y", route[sign]) for sign in route)

    first = (scale_first.astype(jnp.float32)[:, None] * slab_block.astype(jnp.float32)).astype(
        jnp.bfloat16
    )
    scale_rows = jnp.pad(
        jnp.transpose(scale_second.reshape(share, groups))[None], ((0, PAD - 1), (0, 0), (0, col_width - share))
    )
    packed = jnp.concatenate([first.reshape(share, groups, col_width), scale_rows], axis=0)
    packed = lax.all_to_all(packed, ROW, split_axis=1, concat_axis=0, tiled=True)
    joined = jnp.concatenate(near, axis=1)
    packed = after(packed, joined)
    far_near = tuple(lax.ppermute(block, "y", route[sign]) for block, sign in zip(near, route))
    bounds = ((0, SPLIT), (SPLIT, row_count))
    first_keys, second_keys = ((0, -1), (1, 1)), ((1, -1), (0, 1))
    third = {}
    for part, sign in first_keys:
        block = far_near[0 if sign < 0 else 1][slice(*bounds[part])]
        third[part, sign] = lax.ppermute(block, "y", route[sign])
    last = [lax.ppermute(third[part, sign], "y", route[sign]) for part, sign in first_keys]
    packed = packed.reshape(groups, share + PAD, col_width)
    cyclic = packed[:, :share].reshape(row_count, col_width)
    scale_cyclic = packed[:, share, :share].reshape(row_count)

    level_one = butterfly(cyclic[:half], cyclic[half:])
    second = (scale_cyclic.astype(jnp.float32)[:, None] * level_one).astype(jnp.bfloat16)
    stored = jnp.concatenate(
        [
            butterfly(second[:quarter], second[quarter:half]),
            butterfly(second[half : half + quarter], second[half + quarter :]),
        ],
        axis=0,
    ).astype(jnp.bfloat16)

    top_count = PANEL_W // groups // X_HI
    top = stored[: top_count * X_HI].reshape(1, X_HI, top_count, col_width)
    send = jnp.broadcast_to(top, (chips, X_HI, top_count, col_width)).reshape(
        chips * X_HI, top_count, col_width
    )
    got = lax.all_to_all(send, ("chip", "x_hi"), split_axis=0, concat_axis=0)
    for part, sign in second_keys:
        block = after(far_near[0 if sign < 0 else 1], got)[slice(*bounds[part])]
        third[part, sign] = lax.ppermute(block, "y", route[sign])
    twin = lax.ppermute(got, "core", [(0, 1), (1, 0)])
    place = jnp.stack([lax.axis_index(name) for name in ("x_hi", "y", "core")]).astype(jnp.int32)
    swap = [(i, X_HI - 1 - i) for i in range(X_HI)]
    *sums, upper = early_products(
        place,
        got,
        twin,
        stored,
        bounds,
        [0, -1, 1, -2, 2],
        [panel_lower, joined, *far_near],
        [sign * (y_count // 2 - 1) for _, sign in first_keys],
        [third[key] for key in first_keys],
    )
    upper = after(upper, *(third[key] for key in second_keys))
    out = []
    for part, sign in first_keys:
        offsets = [-sign * (y_count // 2 - 1), y_count // 2]
        blocks = [third[part, -sign], last[part]]
        far = last_product(place, upper, sums[2 * part], offsets, blocks, True, jnp.bfloat16, 1)
        came = lax.ppermute(far, "x_hi", swap)
        rest = last_product(place, upper, sums[2 * part + 1], offsets, blocks, False, jnp.float32, -1)
        out.append((rest - came.astype(jnp.float32)).astype(jnp.bfloat16))
    return jnp.concatenate(out, axis=0)


def solution(mesh):
    rows, cols = mesh.devices.shape
    split = Mesh(
        mesh.devices.reshape(rows // CORES, CORES, X_HI, cols // X_HI), ("chip", "core", "x_hi", "y")
    )
    col = ("x_hi", "y")
    placed = (P(ROW, col), P(ROW), P(ROW), P(ROW, col))
    return jax.shard_map(
        per_device, mesh=split, in_specs=placed, out_specs=P(ROW, col), check_vma=False
    )
```

```python
import jax
import jax.numpy as jnp
from jax import lax
from jax.experimental import pallas as pl
from jax.experimental.pallas import tpu as pltpu
from jax.sharding import Mesh, PartitionSpec as P

PANEL_W = 4096
X_HI = 2
CORES = 2
PAD = 8
TILE_M = 256
ROW = ("chip", "core")

inv_root = 0.7071067811865476


def butterfly(top, bottom):
    top = top.astype(jnp.float32)
    bottom = bottom.astype(jnp.float32)
    return jnp.concatenate([(top + bottom) * inv_root, (top - bottom) * inv_root], axis=0)


def after(value, *others):
    return lax.optimization_barrier((value, *others))[0]


VM = pltpu.VMEM


def grant(mib):
    return pltpu.CompilerParams(vmem_limit_bytes=mib << 20)


def whole():
    return pl.BlockSpec(memory_space=VM)


def order_upper(core, got_ref, twin_ref, out_ref):
    pairs, top, width = got_ref.shape
    y_count, depth = out_ref.shape[:2]
    chips, low = pairs // X_HI, top // y_count
    want = lax.broadcasted_iota(jnp.int32, (depth, depth), 0)
    have = lax.broadcasted_iota(jnp.int32, (depth, depth), 1)
    side = (want % CORES + core) % CORES
    source = side * (chips * low) + want // CORES % chips * low + want // (CORES * chips)
    move = jnp.where(source == have, 1.0, 0.0).astype(out_ref.dtype)
    for y in range(y_count):
        for x in range(X_HI):
            pick = [ref[chip * X_HI + x, y * low : (y + 1) * low] for ref in (got_ref, twin_ref) for chip in range(chips)]
            rows = jnp.dot(move, jnp.concatenate(pick, axis=0), preferred_element_type=jnp.float32)
            out_ref[y, :, x * width : (x + 1) * width] = rows.astype(out_ref.dtype)


def early_products(place, got, twin, stored, offsets, blocks, own_offsets, own_blocks):
    rows, width = stored.shape
    y_count = lax.axis_size("y")
    depth, both = blocks[0].shape[1], X_HI * width
    parts = len(own_blocks)
    share = rows // parts
    common = len(offsets) * depth

    def body(place_ref, got_ref, twin_ref, stored_ref, *refs):
        block_refs, own_refs, out_refs = refs[: len(blocks)], refs[len(blocks) : -2 - 2 * parts], refs[-2 - 2 * parts : -2]
        upper_ref, turned = refs[-2:]
        order_upper(place_ref[2], got_ref, twin_ref, upper_ref)
        for n, offset in enumerate(offsets):
            turned[n * depth : (n + 1) * depth] = upper_ref[(place_ref[1] + offset + y_count) % y_count]
        at_left = place_ref[0] == 0

        for part in range(parts):
            turned[common:] = upper_ref[(place_ref[1] + own_offsets[part] + y_count) % y_count]
            far_ref, rest_ref = out_refs[2 * part : 2 * part + 2]

            def one(i, carry):
                local = pl.ds(pl.multiple_of(i * TILE_M, TILE_M), TILE_M)
                full = pl.ds(pl.multiple_of(part * share + i * TILE_M, TILE_M), TILE_M)
                tiles = [ref[full] for ref in block_refs] + [own_refs[part][local]]
                total = jnp.dot(jnp.concatenate(tiles, axis=1), turned[...], preferred_element_type=jnp.float32)
                left, right = total[:, :width], total[:, width:]
                far_ref[local] = jnp.where(at_left, right, left)
                rest_ref[local] = stored_ref[full].astype(jnp.float32) - jnp.where(at_left, left, right)
                return carry

            lax.fori_loop(0, share // TILE_M, one, 0)

    return pl.pallas_call(
        body,
        in_specs=[pl.BlockSpec(memory_space=pltpu.SMEM)] + [whole()] * (3 + len(blocks) + parts),
        out_specs=[whole()] * (2 * parts + 1),
        out_shape=[jax.ShapeDtypeStruct((share, width), jnp.float32)] * (2 * parts)
        + [jax.ShapeDtypeStruct((y_count, depth, both), stored.dtype)],
        scratch_shapes=[VM((common + depth, both), stored.dtype)],
        compiler_params=grant(16),
        name="early_products",
    )(place, got, twin, stored, *blocks, *own_blocks)


def last_product(place, upper, base, offsets, blocks, partner, out_dtype, sign):
    rows, width = base.shape
    y_count = upper.shape[0]

    def body(place_ref, upper_ref, base_ref, *refs):
        *block_refs, out_ref = refs
        side = (place_ref[0] + 1) % X_HI if partner else place_ref[0]
        columns = []
        for offset in offsets:
            both = upper_ref[(place_ref[1] + offset + y_count) % y_count]
            columns.append(jnp.where(side == 0, both[:, :width], both[:, width:]))
        columns = jnp.concatenate(columns, axis=0)
        for start in range(0, rows, TILE_M):
            part = slice(start, start + TILE_M)
            lhs = jnp.concatenate([ref[part] for ref in block_refs], axis=1)
            term = jnp.dot(lhs, columns, preferred_element_type=jnp.float32)
            out_ref[part] = (base_ref[part] + sign * term).astype(out_ref.dtype)

    return pl.pallas_call(
        body,
        in_specs=[pl.BlockSpec(memory_space=pltpu.SMEM)] + [whole()] * (2 + len(blocks)),
        out_specs=whole(),
        out_shape=jax.ShapeDtypeStruct((rows, width), out_dtype),
        compiler_params=grant(8),
        name="last_far" if partner else "last_own",
    )(place, upper, base, *blocks)


def per_device(slab_block, scale_first, scale_second, panel_lower):
    row_count, col_width = slab_block.shape
    chips = lax.axis_size("chip")
    groups = chips * CORES
    y_count = lax.axis_size("y")
    block_width = panel_lower.shape[1]
    share = row_count // groups
    half = row_count // 2
    quarter = row_count // 4

    up = [(i, (i + 1) % y_count) for i in range(y_count)]
    down = [(i, (i - 1) % y_count) for i in range(y_count)]
    route = {-1: up, 1: down}
    near = tuple(lax.ppermute(panel_lower, "y", route[sign]) for sign in route)

    first = (scale_first.astype(jnp.float32)[:, None] * slab_block.astype(jnp.float32)).astype(
        jnp.bfloat16
    )
    scale_rows = jnp.pad(
        jnp.transpose(scale_second.reshape(share, groups))[None], ((0, PAD - 1), (0, 0), (0, col_width - share))
    )
    packed = jnp.concatenate([first.reshape(share, groups, col_width), scale_rows], axis=0)
    packed = lax.all_to_all(packed, ROW, split_axis=1, concat_axis=0, tiled=True)
    joined = jnp.concatenate(near, axis=1)
    packed = after(packed, joined)
    far_near = tuple(lax.ppermute(block, "y", route[sign]) for block, sign in zip(near, route))
    first_keys, second_keys = ((0, -1), (1, 1)), ((1, -1), (0, 1))
    third = {}
    for part, sign in first_keys + second_keys:
        block = far_near[0 if sign < 0 else 1][part * half : (part + 1) * half]
        third[part, sign] = lax.ppermute(block, "y", route[sign])
    last = [lax.ppermute(third[part, sign], "y", route[sign]) for part, sign in first_keys]
    packed = packed.reshape(groups, share + PAD, col_width)
    cyclic = packed[:, :share].reshape(row_count, col_width)
    scale_cyclic = packed[:, share, :share].reshape(row_count)

    level_one = butterfly(cyclic[:half], cyclic[half:])
    second = (scale_cyclic.astype(jnp.float32)[:, None] * level_one).astype(jnp.bfloat16)
    stored = jnp.concatenate(
        [
            butterfly(second[:quarter], second[quarter:half]),
            butterfly(second[half : half + quarter], second[half + quarter :]),
        ],
        axis=0,
    ).astype(jnp.bfloat16)

    top_count = PANEL_W // groups // X_HI
    top = stored[: top_count * X_HI].reshape(1, X_HI, top_count, col_width)
    send = jnp.broadcast_to(top, (chips, X_HI, top_count, col_width)).reshape(
        chips * X_HI, top_count, col_width
    )
    got = lax.all_to_all(send, ("chip", "x_hi"), split_axis=0, concat_axis=0)
    got = after(got, third[0, -1])
    twin = lax.ppermute(got, "core", [(0, 1), (1, 0)])
    twin = after(twin, third[1, -1])
    place = jnp.stack([lax.axis_index(name) for name in ("x_hi", "y", "core")]).astype(jnp.int32)
    swap = [(i, X_HI - 1 - i) for i in range(X_HI)]
    *sums, upper = early_products(
        place,
        got,
        twin,
        stored,
        [0, -1, 1, -2, 2],
        [panel_lower, joined, *far_near],
        [sign * (y_count // 2 - 1) for _, sign in first_keys],
        [third[key] for key in first_keys],
    )
    out = []
    for part, sign in first_keys:
        offsets = [-sign * (y_count // 2 - 1), y_count // 2]
        blocks = [third[part, -sign], last[part]]
        far = last_product(place, upper, sums[2 * part], offsets, blocks, True, jnp.bfloat16, 1)
        came = lax.ppermute(far, "x_hi", swap)
        rest = last_product(place, upper, sums[2 * part + 1], offsets, blocks, False, jnp.float32, -1)
        out.append((rest - came.astype(jnp.float32)).astype(jnp.bfloat16))
    return jnp.concatenate(out, axis=0)


def solution(mesh):
    rows, cols = mesh.devices.shape
    split = Mesh(
        mesh.devices.reshape(rows // CORES, CORES, X_HI, cols // X_HI), ("chip", "core", "x_hi", "y")
    )
    col = ("x_hi", "y")
    placed = (P(ROW, col), P(ROW), P(ROW), P(ROW, col))
    return jax.shard_map(
        per_device, mesh=split, in_specs=placed, out_specs=P(ROW, col), check_vma=False
    )
```

```python
import jax
import jax.numpy as jnp
from jax import lax
from jax.experimental import pallas as pl
from jax.experimental.pallas import tpu as pltpu
from jax.sharding import Mesh, PartitionSpec as P

PANEL_W = 4096
X_HI = 2
CORES = 2
PAD = 8
TILE_M = 256
SPLIT = 1280
ROW = ("chip", "core")

inv_root = 0.7071067811865476


def butterfly(top, bottom):
    top = top.astype(jnp.float32)
    bottom = bottom.astype(jnp.float32)
    return jnp.concatenate([(top + bottom) * inv_root, (top - bottom) * inv_root], axis=0)


def after(value, *others):
    return lax.optimization_barrier((value, *others))[0]


VM = pltpu.VMEM


def grant(mib):
    return pltpu.CompilerParams(vmem_limit_bytes=mib << 20)


def whole():
    return pl.BlockSpec(memory_space=VM)


def order_upper(core, got_ref, twin_ref, out_ref):
    pairs, top, width = got_ref.shape
    y_count, depth = out_ref.shape[:2]
    chips, low = pairs // X_HI, top // y_count
    want = lax.broadcasted_iota(jnp.int32, (depth, depth), 0)
    have = lax.broadcasted_iota(jnp.int32, (depth, depth), 1)
    side = (want % CORES + core) % CORES
    source = side * (chips * low) + want // CORES % chips * low + want // (CORES * chips)
    move = jnp.where(source == have, 1.0, 0.0).astype(out_ref.dtype)
    for y in range(y_count):
        for x in range(X_HI):
            pick = [ref[chip * X_HI + x, y * low : (y + 1) * low] for ref in (got_ref, twin_ref) for chip in range(chips)]
            rows = jnp.dot(move, jnp.concatenate(pick, axis=0), preferred_element_type=jnp.float32)
            out_ref[y, :, x * width : (x + 1) * width] = rows.astype(out_ref.dtype)


def early_products(place, got, twin, stored, bounds, offsets, blocks, own_offset, own_block):
    rows, width = stored.shape
    y_count = lax.axis_size("y")
    depth, both = blocks[0].shape[1], X_HI * width
    parts = len(bounds)
    common = len(offsets) * depth

    def body(place_ref, got_ref, twin_ref, stored_ref, *refs):
        block_refs, own_ref, out_refs = refs[: len(blocks)], refs[len(blocks)], refs[len(blocks) + 1 : -2]
        upper_ref, turned = refs[-2:]
        order_upper(place_ref[2], got_ref, twin_ref, upper_ref)
        for n, offset in enumerate(offsets):
            turned[n * depth : (n + 1) * depth] = upper_ref[(place_ref[1] + offset + y_count) % y_count]
        turned[common:] = upper_ref[(place_ref[1] + own_offset + y_count) % y_count]
        at_left = place_ref[0] == 0

        for part, (start, stop) in enumerate(bounds):
            far_ref, rest_ref = out_refs[2 * part : 2 * part + 2]

            def one(i, carry):
                local = pl.ds(pl.multiple_of(i * TILE_M, TILE_M), TILE_M)
                full = pl.ds(pl.multiple_of(start + i * TILE_M, TILE_M), TILE_M)
                tiles = [ref[full] for ref in block_refs]
                if part == 0:
                    tiles.append(own_ref[local])
                depth_here = sum(tile.shape[1] for tile in tiles)
                total = jnp.dot(jnp.concatenate(tiles, axis=1), turned[:depth_here], preferred_element_type=jnp.float32)
                left, right = total[:, :width], total[:, width:]
                far_ref[local] = jnp.where(at_left, right, left)
                rest_ref[local] = stored_ref[full].astype(jnp.float32) - jnp.where(at_left, left, right)
                return carry

            lax.fori_loop(0, (stop - start) // TILE_M, one, 0)

    return pl.pallas_call(
        body,
        in_specs=[pl.BlockSpec(memory_space=pltpu.SMEM)] + [whole()] * (4 + len(blocks)),
        out_specs=[whole()] * (2 * parts + 1),
        out_shape=[jax.ShapeDtypeStruct((b - a, width), jnp.float32) for a, b in bounds for _ in range(2)]
        + [jax.ShapeDtypeStruct((y_count, depth, both), stored.dtype)],
        scratch_shapes=[VM((common + depth, both), stored.dtype)],
        compiler_params=grant(16),
        name="early_products",
    )(place, got, twin, stored, *blocks, own_block)


def last_product(place, upper, base, offsets, blocks, bases, partner, out_dtype, sign):
    rows, width = base.shape
    y_count = upper.shape[0]

    def body(place_ref, upper_ref, base_ref, *refs):
        *block_refs, out_ref = refs
        side = (place_ref[0] + 1) % X_HI if partner else place_ref[0]
        columns = []
        for offset in offsets:
            both = upper_ref[(place_ref[1] + offset + y_count) % y_count]
            columns.append(jnp.where(side == 0, both[:, :width], both[:, width:]))
        columns = jnp.concatenate(columns, axis=0)
        for start in range(0, rows, TILE_M):
            part = slice(start, start + TILE_M)
            tiles = [ref[at + start : at + start + TILE_M] for ref, at in zip(block_refs, bases)]
            lhs = jnp.concatenate(tiles, axis=1)
            term = jnp.dot(lhs, columns, preferred_element_type=jnp.float32)
            out_ref[part] = (base_ref[part] + sign * term).astype(out_ref.dtype)

    return pl.pallas_call(
        body,
        in_specs=[pl.BlockSpec(memory_space=pltpu.SMEM)] + [whole()] * (2 + len(blocks)),
        out_specs=whole(),
        out_shape=jax.ShapeDtypeStruct((rows, width), out_dtype),
        compiler_params=grant(8),
        name="last_far" if partner else "last_own",
    )(place, upper, base, *blocks)


def per_device(slab_block, scale_first, scale_second, panel_lower):
    row_count, col_width = slab_block.shape
    chips = lax.axis_size("chip")
    groups = chips * CORES
    y_count = lax.axis_size("y")
    block_width = panel_lower.shape[1]
    share = row_count // groups
    half = row_count // 2
    quarter = row_count // 4

    up = [(i, (i + 1) % y_count) for i in range(y_count)]
    down = [(i, (i - 1) % y_count) for i in range(y_count)]
    route = {-1: up, 1: down}
    near = tuple(lax.ppermute(panel_lower, "y", route[sign]) for sign in route)

    first = (scale_first.astype(jnp.float32)[:, None] * slab_block.astype(jnp.float32)).astype(
        jnp.bfloat16
    )
    scale_rows = jnp.pad(
        jnp.transpose(scale_second.reshape(share, groups))[None], ((0, PAD - 1), (0, 0), (0, col_width - share))
    )
    packed = jnp.concatenate([first.reshape(share, groups, col_width), scale_rows], axis=0)
    packed = lax.all_to_all(packed, ROW, split_axis=1, concat_axis=0, tiled=True)
    joined = jnp.concatenate(near, axis=1)
    packed = after(packed, joined)
    far_near = tuple(lax.ppermute(block, "y", route[sign]) for block, sign in zip(near, route))
    bounds = ((0, SPLIT), (SPLIT, row_count))
    rising = [lax.ppermute(far_near[0][start:stop], "y", up) for start, stop in bounds]
    falling = lax.ppermute(far_near[1], "y", down)
    last = [lax.ppermute(rising[0], "y", up)]
    packed = packed.reshape(groups, share + PAD, col_width)
    cyclic = packed[:, :share].reshape(row_count, col_width)
    scale_cyclic = packed[:, share, :share].reshape(row_count)

    level_one = butterfly(cyclic[:half], cyclic[half:])
    second = (scale_cyclic.astype(jnp.float32)[:, None] * level_one).astype(jnp.bfloat16)
    stored = jnp.concatenate(
        [
            butterfly(second[:quarter], second[quarter:half]),
            butterfly(second[half : half + quarter], second[half + quarter :]),
        ],
        axis=0,
    ).astype(jnp.bfloat16)

    top_count = PANEL_W // groups // X_HI
    top = stored[: top_count * X_HI].reshape(1, X_HI, top_count, col_width)
    send = jnp.broadcast_to(top, (chips, X_HI, top_count, col_width)).reshape(
        chips * X_HI, top_count, col_width
    )
    got = lax.all_to_all(send, ("chip", "x_hi"), split_axis=0, concat_axis=0)
    twin = lax.ppermute(got, "core", [(0, 1), (1, 0)])
    place = jnp.stack([lax.axis_index(name) for name in ("x_hi", "y", "core")]).astype(jnp.int32)
    swap = [(i, X_HI - 1 - i) for i in range(X_HI)]
    *sums, upper = early_products(
        place,
        got,
        twin,
        stored,
        bounds,
        [0, -1, 1, -2, 2],
        [panel_lower, joined, *far_near],
        1 - y_count // 2,
        rising[0],
    )
    last.append(lax.ppermute(after(falling, upper)[SPLIT:], "y", down))
    out = []
    offsets = [y_count // 2 - 1, y_count // 2]
    for part, (start, _) in enumerate(bounds):
        blocks, bases, late = [falling, last[part]], [start, 0], []
        if part:
            blocks, bases, late = [*blocks, rising[part]], [*bases, 0], [1 - y_count // 2]
        far = last_product(place, upper, sums[2 * part], offsets + late, blocks, bases, True, jnp.bfloat16, 1)
        came = lax.ppermute(far, "x_hi", swap)
        rest = last_product(place, upper, sums[2 * part + 1], offsets + late, blocks, bases, False, jnp.float32, -1)
        out.append((rest - came.astype(jnp.float32)).astype(jnp.bfloat16))
    return jnp.concatenate(out, axis=0)


def solution(mesh):
    rows, cols = mesh.devices.shape
    split = Mesh(
        mesh.devices.reshape(rows // CORES, CORES, X_HI, cols // X_HI), ("chip", "core", "x_hi", "y")
    )
    col = ("x_hi", "y")
    placed = (P(ROW, col), P(ROW), P(ROW), P(ROW, col))
    return jax.shard_map(
        per_device, mesh=split, in_specs=placed, out_specs=P(ROW, col), check_vma=False
    )
```

```python
import jax
import jax.numpy as jnp
from jax import lax
from jax.experimental import pallas as pl
from jax.experimental.pallas import tpu as pltpu
from jax.sharding import Mesh, PartitionSpec as P

PANEL_W = 4096
X_HI = 2
CORES = 2
PAD = 8
TILE_M = 256
SPLIT = 1280
ROW = ("chip", "core")

inv_root = 0.7071067811865476


def after(value, *others):
    return lax.optimization_barrier((value, *others))[0]


VM = pltpu.VMEM


def grant(mib):
    return pltpu.CompilerParams(vmem_limit_bytes=mib << 20)


def whole():
    return pl.BlockSpec(memory_space=VM)


def butterflies(packed, share, chips, top_count):
    groups, _, width = packed.shape
    quarter = groups // 4
    rows = groups * share

    def body(packed_ref, stored_ref, send_ref):
        scale = jnp.transpose(packed_ref[:, share, :].astype(jnp.float32))
        for d in range(quarter):
            at = [d + n * quarter for n in range(4)]
            one = [packed_ref[n, :share].astype(jnp.float32) for n in at]
            two = [one[0] + one[2], one[1] + one[3], one[0] - one[2], one[1] - one[3]]
            two = [
                (scale[:share, n : n + 1] * (value * inv_root)).astype(packed.dtype).astype(jnp.float32)
                for n, value in zip(at, two)
            ]
            out = [two[0] + two[1], two[0] - two[1], two[2] + two[3], two[2] - two[3]]
            for n, value in zip(at, out):
                stored_ref[n * share : (n + 1) * share] = (value * inv_root).astype(packed.dtype)
        for x in range(X_HI):
            top = stored_ref[x * top_count : (x + 1) * top_count]
            for chip in range(chips):
                send_ref[chip * X_HI + x] = top

    return pl.pallas_call(
        body,
        in_specs=[whole()],
        out_specs=[whole(), whole()],
        out_shape=[
            jax.ShapeDtypeStruct((rows, width), packed.dtype),
            jax.ShapeDtypeStruct((chips * X_HI, top_count, width), packed.dtype),
        ],
        compiler_params=grant(8),
        name="butterflies",
    )(packed)


def order_upper(core, got_ref, twin_ref, out_ref):
    pairs, top, width = got_ref.shape
    y_count, depth = out_ref.shape[:2]
    chips, low = pairs // X_HI, top // y_count
    want = lax.broadcasted_iota(jnp.int32, (depth, depth), 0)
    have = lax.broadcasted_iota(jnp.int32, (depth, depth), 1)
    side = (want % CORES + core) % CORES
    source = side * (chips * low) + want // CORES % chips * low + want // (CORES * chips)
    move = jnp.where(source == have, 1.0, 0.0).astype(out_ref.dtype)
    for y in range(y_count):
        for x in range(X_HI):
            pick = [ref[chip * X_HI + x, y * low : (y + 1) * low] for ref in (got_ref, twin_ref) for chip in range(chips)]
            rows = jnp.dot(move, jnp.concatenate(pick, axis=0), preferred_element_type=jnp.float32)
            out_ref[y, :, x * width : (x + 1) * width] = rows.astype(out_ref.dtype)


def early_products(place, got, twin, stored, bounds, offsets, blocks, own_offset, own_block):
    rows, width = stored.shape
    y_count = lax.axis_size("y")
    depth, both = blocks[0].shape[1], X_HI * width
    parts = len(bounds)
    common = len(offsets) * depth

    def body(place_ref, got_ref, twin_ref, stored_ref, *refs):
        block_refs, own_ref, out_refs = refs[: len(blocks)], refs[len(blocks)], refs[len(blocks) + 1 : -2]
        upper_ref, turned = refs[-2:]
        order_upper(place_ref[2], got_ref, twin_ref, upper_ref)
        for n, offset in enumerate(offsets):
            turned[n * depth : (n + 1) * depth] = upper_ref[(place_ref[1] + offset + y_count) % y_count]
        turned[common:] = upper_ref[(place_ref[1] + own_offset + y_count) % y_count]
        at_left = place_ref[0] == 0

        for part, (start, stop) in enumerate(bounds):
            far_ref, rest_ref = out_refs[2 * part : 2 * part + 2]

            def one(i, carry):
                local = pl.ds(pl.multiple_of(i * TILE_M, TILE_M), TILE_M)
                full = pl.ds(pl.multiple_of(start + i * TILE_M, TILE_M), TILE_M)
                tiles = [ref[full] for ref in block_refs]
                if part == 0:
                    tiles.append(own_ref[local])
                depth_here = sum(tile.shape[1] for tile in tiles)
                total = jnp.dot(jnp.concatenate(tiles, axis=1), turned[:depth_here], preferred_element_type=jnp.float32)
                left, right = total[:, :width], total[:, width:]
                far_ref[local] = jnp.where(at_left, right, left)
                rest_ref[local] = stored_ref[full].astype(jnp.float32) - jnp.where(at_left, left, right)
                return carry

            lax.fori_loop(0, (stop - start) // TILE_M, one, 0)

    return pl.pallas_call(
        body,
        in_specs=[pl.BlockSpec(memory_space=pltpu.SMEM)] + [whole()] * (4 + len(blocks)),
        out_specs=[whole()] * (2 * parts + 1),
        out_shape=[jax.ShapeDtypeStruct((b - a, width), jnp.float32) for a, b in bounds for _ in range(2)]
        + [jax.ShapeDtypeStruct((y_count, depth, both), stored.dtype)],
        scratch_shapes=[VM((common + depth, both), stored.dtype)],
        compiler_params=grant(16),
        name="early_products",
    )(place, got, twin, stored, *blocks, own_block)


def last_product(place, upper, base, offsets, blocks, bases, partner, out_dtype, sign):
    rows, width = base.shape
    y_count = upper.shape[0]

    def body(place_ref, upper_ref, base_ref, *refs):
        *block_refs, out_ref = refs
        side = (place_ref[0] + 1) % X_HI if partner else place_ref[0]
        columns = []
        for offset in offsets:
            both = upper_ref[(place_ref[1] + offset + y_count) % y_count]
            columns.append(jnp.where(side == 0, both[:, :width], both[:, width:]))
        columns = jnp.concatenate(columns, axis=0)
        for start in range(0, rows, TILE_M):
            part = slice(start, start + TILE_M)
            tiles = [ref[at + start : at + start + TILE_M] for ref, at in zip(block_refs, bases)]
            lhs = jnp.concatenate(tiles, axis=1)
            term = jnp.dot(lhs, columns, preferred_element_type=jnp.float32)
            out_ref[part] = (base_ref[part] + sign * term).astype(out_ref.dtype)

    return pl.pallas_call(
        body,
        in_specs=[pl.BlockSpec(memory_space=pltpu.SMEM)] + [whole()] * (2 + len(blocks)),
        out_specs=whole(),
        out_shape=jax.ShapeDtypeStruct((rows, width), out_dtype),
        compiler_params=grant(8),
        name="last_far" if partner else "last_own",
    )(place, upper, base, *blocks)


def per_device(slab_block, scale_first, scale_second, panel_lower):
    row_count, col_width = slab_block.shape
    chips = lax.axis_size("chip")
    groups = chips * CORES
    y_count = lax.axis_size("y")
    block_width = panel_lower.shape[1]
    share = row_count // groups

    up = [(i, (i + 1) % y_count) for i in range(y_count)]
    down = [(i, (i - 1) % y_count) for i in range(y_count)]
    route = {-1: up, 1: down}
    near = tuple(lax.ppermute(panel_lower, "y", route[sign]) for sign in route)

    first = (scale_first.astype(jnp.float32)[:, None] * slab_block.astype(jnp.float32)).astype(
        jnp.bfloat16
    )
    scale_rows = jnp.pad(
        jnp.transpose(scale_second.reshape(share, groups))[None], ((0, PAD - 1), (0, 0), (0, col_width - share))
    )
    packed = jnp.concatenate([first.reshape(share, groups, col_width), scale_rows], axis=0)
    packed = lax.all_to_all(packed, ROW, split_axis=1, concat_axis=0, tiled=True)
    joined = jnp.concatenate(near, axis=1)
    packed = after(packed, joined)
    far_near = tuple(lax.ppermute(block, "y", route[sign]) for block, sign in zip(near, route))
    bounds = ((0, SPLIT), (SPLIT, row_count))
    rising = [lax.ppermute(far_near[0][start:stop], "y", up) for start, stop in bounds]
    falling = lax.ppermute(far_near[1], "y", down)
    last = [lax.ppermute(rising[0], "y", up)]
    packed = packed.reshape(groups, share + PAD, col_width)
    top_count = PANEL_W // groups // X_HI
    stored, send = butterflies(packed, share, chips, top_count)
    got = lax.all_to_all(send, ("chip", "x_hi"), split_axis=0, concat_axis=0)
    twin = lax.ppermute(got, "core", [(0, 1), (1, 0)])
    place = jnp.stack([lax.axis_index(name) for name in ("x_hi", "y", "core")]).astype(jnp.int32)
    swap = [(i, X_HI - 1 - i) for i in range(X_HI)]
    *sums, upper = early_products(
        place,
        got,
        twin,
        stored,
        bounds,
        [0, -1, 1, -2, 2],
        [panel_lower, joined, *far_near],
        1 - y_count // 2,
        rising[0],
    )
    last.append(lax.ppermute(after(falling, upper)[SPLIT:], "y", down))
    out = []
    offsets = [y_count // 2 - 1, y_count // 2]
    for part, (start, _) in enumerate(bounds):
        blocks, bases, late = [falling, last[part]], [start, 0], []
        if part:
            blocks, bases, late = [*blocks, rising[part]], [*bases, 0], [1 - y_count // 2]
        far = last_product(place, upper, sums[2 * part], offsets + late, blocks, bases, True, jnp.bfloat16, 1)
        came = lax.ppermute(far, "x_hi", swap)
        rest = last_product(place, upper, sums[2 * part + 1], offsets + late, blocks, bases, False, jnp.float32, -1)
        out.append((rest - came.astype(jnp.float32)).astype(jnp.bfloat16))
    return jnp.concatenate(out, axis=0)


def solution(mesh):
    rows, cols = mesh.devices.shape
    split = Mesh(
        mesh.devices.reshape(rows // CORES, CORES, X_HI, cols // X_HI), ("chip", "core", "x_hi", "y")
    )
    col = ("x_hi", "y")
    placed = (P(ROW, col), P(ROW), P(ROW), P(ROW, col))
    return jax.shard_map(
        per_device, mesh=split, in_specs=placed, out_specs=P(ROW, col), check_vma=False
    )
```

```python
import jax
import jax.numpy as jnp
from jax import lax
from jax.experimental import pallas as pl
from jax.experimental.pallas import tpu as pltpu
from jax.sharding import Mesh, PartitionSpec as P

PANEL_W = 4096
X_HI = 2
CORES = 2
PAD = 8
TILE_M = 256
SPLIT = 1280
ROW = ("chip", "core")

inv_root = 0.7071067811865476


def after(value, *others):
    return lax.optimization_barrier((value, *others))[0]


VM = pltpu.VMEM


def grant(mib):
    return pltpu.CompilerParams(vmem_limit_bytes=mib << 20)


def whole():
    return pl.BlockSpec(memory_space=VM)


def butterflies(packed, share, chips, top_count):
    groups, _, width = packed.shape
    quarter = groups // 4
    rows = groups * share

    def body(packed_ref, stored_ref, send_ref):
        scale = jnp.transpose(packed_ref[:, share, :].astype(jnp.float32))
        for d in range(quarter):
            at = [d + n * quarter for n in range(4)]
            one = [packed_ref[n, :share].astype(jnp.float32) for n in at]
            two = [one[0] + one[2], one[1] + one[3], one[0] - one[2], one[1] - one[3]]
            two = [
                (scale[:share, n : n + 1] * (value * inv_root)).astype(packed.dtype).astype(jnp.float32)
                for n, value in zip(at, two)
            ]
            out = [two[0] + two[1], two[0] - two[1], two[2] + two[3], two[2] - two[3]]
            for n, value in zip(at, out):
                stored_ref[n * share : (n + 1) * share] = (value * inv_root).astype(packed.dtype)
        for x in range(X_HI):
            top = stored_ref[x * top_count : (x + 1) * top_count]
            for chip in range(chips):
                send_ref[chip * X_HI + x] = top

    return pl.pallas_call(
        body,
        in_specs=[whole()],
        out_specs=[whole(), whole()],
        out_shape=[
            jax.ShapeDtypeStruct((rows, width), packed.dtype),
            jax.ShapeDtypeStruct((chips * X_HI, top_count, width), packed.dtype),
        ],
        compiler_params=grant(8),
        name="butterflies",
    )(packed)


def order_upper(core, got_ref, twin_ref, out_ref):
    pairs, top, width = got_ref.shape
    y_count, depth = out_ref.shape[:2]
    chips, low = pairs // X_HI, top // y_count
    want = lax.broadcasted_iota(jnp.int32, (depth, depth), 0)
    have = lax.broadcasted_iota(jnp.int32, (depth, depth), 1)
    side = (want % CORES + core) % CORES
    source = side * (chips * low) + want // CORES % chips * low + want // (CORES * chips)
    move = jnp.where(source == have, 1.0, 0.0).astype(out_ref.dtype)
    for y in range(y_count):
        for x in range(X_HI):
            pick = [ref[chip * X_HI + x, y * low : (y + 1) * low] for ref in (got_ref, twin_ref) for chip in range(chips)]
            rows = jnp.dot(move, jnp.concatenate(pick, axis=0), preferred_element_type=jnp.float32)
            out_ref[y, :, x * width : (x + 1) * width] = rows.astype(out_ref.dtype)


def early_products(place, got, twin, stored, bounds, offsets, blocks, own_offset, own_block):
    rows, width = stored.shape
    y_count = lax.axis_size("y")
    depth, both = blocks[0].shape[1], X_HI * width
    parts = len(bounds)
    common = len(offsets) * depth
    starts = [sum(block.shape[1] for block in blocks[:n]) for n in range(len(blocks))]

    def body(place_ref, got_ref, twin_ref, stored_ref, *refs):
        block_refs, own_ref, out_refs = refs[: len(blocks)], refs[len(blocks)], refs[len(blocks) + 1 : -4]
        upper_ref, turned, here, arrived = refs[-4:]
        copies = [
            pltpu.make_async_copy(ref, here.at[:, at : at + ref.shape[1]], arrived.at[n])
            for n, (ref, at) in enumerate(zip(block_refs, starts))
        ]
        for copy in copies:
            copy.start()
        order_upper(place_ref[2], got_ref, twin_ref, upper_ref)
        for n, offset in enumerate(offsets):
            turned[n * depth : (n + 1) * depth] = upper_ref[(place_ref[1] + offset + y_count) % y_count]
        turned[common:] = upper_ref[(place_ref[1] + own_offset + y_count) % y_count]
        at_left = place_ref[0] == 0
        for copy in copies:
            copy.wait()

        for part, (start, stop) in enumerate(bounds):
            far_ref, rest_ref = out_refs[2 * part : 2 * part + 2]

            def one(i, carry):
                local = pl.ds(pl.multiple_of(i * TILE_M, TILE_M), TILE_M)
                full = pl.ds(pl.multiple_of(start + i * TILE_M, TILE_M), TILE_M)
                tiles = [here[full]]
                if part == 0:
                    tiles.append(own_ref[local])
                depth_here = sum(tile.shape[1] for tile in tiles)
                total = jnp.dot(jnp.concatenate(tiles, axis=1), turned[:depth_here], preferred_element_type=jnp.float32)
                left, right = total[:, :width], total[:, width:]
                far_ref[local] = jnp.where(at_left, right, left)
                rest_ref[local] = stored_ref[full].astype(jnp.float32) - jnp.where(at_left, left, right)
                return carry

            lax.fori_loop(0, (stop - start) // TILE_M, one, 0)

    return pl.pallas_call(
        body,
        in_specs=[pl.BlockSpec(memory_space=pltpu.SMEM)]
        + [whole()] * 3
        + [pl.BlockSpec(memory_space=pltpu.HBM)] * len(blocks)
        + [whole()],
        out_specs=[whole()] * (2 * parts + 1),
        out_shape=[jax.ShapeDtypeStruct((b - a, width), jnp.float32) for a, b in bounds for _ in range(2)]
        + [jax.ShapeDtypeStruct((y_count, depth, both), stored.dtype)],
        scratch_shapes=[
            VM((common + depth, both), stored.dtype),
            VM((rows, common), stored.dtype),
            pltpu.SemaphoreType.DMA((len(blocks),)),
        ],
        compiler_params=grant(48),
        name="early_products",
    )(place, got, twin, stored, *blocks, own_block)


def last_product(place, upper, base, offsets, blocks, bases, partner, out_dtype, sign):
    rows, width = base.shape
    y_count = upper.shape[0]

    def body(place_ref, upper_ref, base_ref, *refs):
        *block_refs, out_ref = refs
        side = (place_ref[0] + 1) % X_HI if partner else place_ref[0]
        columns = []
        for offset in offsets:
            both = upper_ref[(place_ref[1] + offset + y_count) % y_count]
            columns.append(jnp.where(side == 0, both[:, :width], both[:, width:]))
        columns = jnp.concatenate(columns, axis=0)
        for start in range(0, rows, TILE_M):
            part = slice(start, start + TILE_M)
            tiles = [ref[at + start : at + start + TILE_M] for ref, at in zip(block_refs, bases)]
            lhs = jnp.concatenate(tiles, axis=1)
            term = jnp.dot(lhs, columns, preferred_element_type=jnp.float32)
            out_ref[part] = (base_ref[part] + sign * term).astype(out_ref.dtype)

    return pl.pallas_call(
        body,
        in_specs=[pl.BlockSpec(memory_space=pltpu.SMEM)] + [whole()] * (2 + len(blocks)),
        out_specs=whole(),
        out_shape=jax.ShapeDtypeStruct((rows, width), out_dtype),
        compiler_params=grant(8),
        name="last_far" if partner else "last_own",
    )(place, upper, base, *blocks)


def per_device(slab_block, scale_first, scale_second, panel_lower):
    row_count, col_width = slab_block.shape
    chips = lax.axis_size("chip")
    groups = chips * CORES
    y_count = lax.axis_size("y")
    block_width = panel_lower.shape[1]
    share = row_count // groups

    up = [(i, (i + 1) % y_count) for i in range(y_count)]
    down = [(i, (i - 1) % y_count) for i in range(y_count)]
    route = {-1: up, 1: down}
    near = tuple(lax.ppermute(panel_lower, "y", route[sign]) for sign in route)

    first = (scale_first.astype(jnp.float32)[:, None] * slab_block.astype(jnp.float32)).astype(
        jnp.bfloat16
    )
    scale_rows = jnp.pad(
        jnp.transpose(scale_second.reshape(share, groups))[None], ((0, PAD - 1), (0, 0), (0, col_width - share))
    )
    packed = jnp.concatenate([first.reshape(share, groups, col_width), scale_rows], axis=0)
    packed = lax.all_to_all(packed, ROW, split_axis=1, concat_axis=0, tiled=True)
    joined = jnp.concatenate(near, axis=1)
    packed = after(packed, joined)
    far_near = tuple(lax.ppermute(block, "y", route[sign]) for block, sign in zip(near, route))
    bounds = ((0, SPLIT), (SPLIT, row_count))
    rising = [lax.ppermute(far_near[0][start:stop], "y", up) for start, stop in bounds]
    falling = lax.ppermute(far_near[1], "y", down)
    last = [lax.ppermute(rising[0], "y", up)]
    packed = packed.reshape(groups, share + PAD, col_width)
    top_count = PANEL_W // groups // X_HI
    stored, send = butterflies(packed, share, chips, top_count)
    got = lax.all_to_all(send, ("chip", "x_hi"), split_axis=0, concat_axis=0)
    twin = lax.ppermute(got, "core", [(0, 1), (1, 0)])
    place = jnp.stack([lax.axis_index(name) for name in ("x_hi", "y", "core")]).astype(jnp.int32)
    swap = [(i, X_HI - 1 - i) for i in range(X_HI)]
    *sums, upper = early_products(
        place,
        got,
        twin,
        stored,
        bounds,
        [0, -1, 1, -2, 2],
        [panel_lower, joined, *far_near],
        1 - y_count // 2,
        rising[0],
    )
    last.append(lax.ppermute(after(falling, upper)[SPLIT:], "y", down))
    out = []
    offsets = [y_count // 2 - 1, y_count // 2]
    for part, (start, _) in enumerate(bounds):
        blocks, bases, late = [falling, last[part]], [start, 0], []
        if part:
            blocks, bases, late = [*blocks, rising[part]], [*bases, 0], [1 - y_count // 2]
        far = last_product(place, upper, sums[2 * part], offsets + late, blocks, bases, True, jnp.bfloat16, 1)
        came = lax.ppermute(far, "x_hi", swap)
        rest = last_product(place, upper, sums[2 * part + 1], offsets + late, blocks, bases, False, jnp.float32, -1)
        out.append((rest - came.astype(jnp.float32)).astype(jnp.bfloat16))
    return jnp.concatenate(out, axis=0)


def solution(mesh):
    rows, cols = mesh.devices.shape
    split = Mesh(
        mesh.devices.reshape(rows // CORES, CORES, X_HI, cols // X_HI), ("chip", "core", "x_hi", "y")
    )
    col = ("x_hi", "y")
    placed = (P(ROW, col), P(ROW), P(ROW), P(ROW, col))
    return jax.shard_map(
        per_device, mesh=split, in_specs=placed, out_specs=P(ROW, col), check_vma=False
    )
```

```python
import jax
import jax.numpy as jnp
from jax import lax
from jax.experimental import pallas as pl
from jax.experimental.pallas import tpu as pltpu
from jax.sharding import Mesh, PartitionSpec as P

PANEL_W = 4096
X_HI = 2
CORES = 2
PAD = 8
TILE_M = 256
SPLIT = 1280
ROW = ("chip", "core")

inv_root = 0.7071067811865476


def after(value, *others):
    return lax.optimization_barrier((value, *others))[0]


VM = pltpu.VMEM


def grant(mib):
    return pltpu.CompilerParams(vmem_limit_bytes=mib << 20)


def whole():
    return pl.BlockSpec(memory_space=VM)


def butterflies(packed, share, chips, top_count):
    groups, _, width = packed.shape
    quarter = groups // 4
    rows = groups * share

    def body(packed_ref, stored_ref, send_ref):
        scale = jnp.transpose(packed_ref[:, share, :].astype(jnp.float32))
        for d in range(quarter):
            at = [d + n * quarter for n in range(4)]
            one = [packed_ref[n, :share].astype(jnp.float32) for n in at]
            two = [one[0] + one[2], one[1] + one[3], one[0] - one[2], one[1] - one[3]]
            two = [
                (scale[:share, n : n + 1] * (value * inv_root)).astype(packed.dtype).astype(jnp.float32)
                for n, value in zip(at, two)
            ]
            out = [two[0] + two[1], two[0] - two[1], two[2] + two[3], two[2] - two[3]]
            for n, value in zip(at, out):
                stored_ref[n * share : (n + 1) * share] = (value * inv_root).astype(packed.dtype)
        for x in range(X_HI):
            top = stored_ref[x * top_count : (x + 1) * top_count]
            for chip in range(chips):
                send_ref[chip * X_HI + x] = top

    return pl.pallas_call(
        body,
        in_specs=[whole()],
        out_specs=[whole(), whole()],
        out_shape=[
            jax.ShapeDtypeStruct((rows, width), packed.dtype),
            jax.ShapeDtypeStruct((chips * X_HI, top_count, width), packed.dtype),
        ],
        compiler_params=grant(8),
        name="butterflies",
    )(packed)


def order_upper(core, got_ref, twin_ref, out_ref):
    pairs, top, width = got_ref.shape
    y_count, depth = out_ref.shape[:2]
    chips, low = pairs // X_HI, top // y_count
    want = lax.broadcasted_iota(jnp.int32, (depth, depth), 0)
    have = lax.broadcasted_iota(jnp.int32, (depth, depth), 1)
    side = (want % CORES + core) % CORES
    source = side * (chips * low) + want // CORES % chips * low + want // (CORES * chips)
    move = jnp.where(source == have, 1.0, 0.0).astype(out_ref.dtype)
    for y in range(y_count):
        for x in range(X_HI):
            pick = [ref[chip * X_HI + x, y * low : (y + 1) * low] for ref in (got_ref, twin_ref) for chip in range(chips)]
            rows = jnp.dot(move, jnp.concatenate(pick, axis=0), preferred_element_type=jnp.float32)
            out_ref[y, :, x * width : (x + 1) * width] = rows.astype(out_ref.dtype)


def early_products(place, got, twin, stored, bounds, offsets, blocks, own_offset, own_block):
    rows, width = stored.shape
    y_count = lax.axis_size("y")
    depth, both = blocks[0].shape[1], X_HI * width
    parts = len(bounds)
    common = len(offsets) * depth
    starts = [sum(block.shape[1] for block in blocks[:n]) for n in range(len(blocks))]

    def body(place_ref, got_ref, twin_ref, stored_ref, *refs):
        block_refs, own_ref, out_refs = refs[: len(blocks)], refs[len(blocks)], refs[len(blocks) + 1 : -4]
        upper_ref, turned, here, arrived = refs[-4:]
        copies = [
            [
                pltpu.make_async_copy(
                    ref.at[start:stop], here.at[start:stop, at : at + ref.shape[1]], arrived.at[part * len(blocks) + n]
                )
                for n, (ref, at) in enumerate(zip(block_refs, starts))
            ]
            for part, (start, stop) in enumerate(bounds)
        ]
        for copy in sum(copies, []):
            copy.start()
        order_upper(place_ref[2], got_ref, twin_ref, upper_ref)
        for n, offset in enumerate(offsets):
            turned[n * depth : (n + 1) * depth] = upper_ref[(place_ref[1] + offset + y_count) % y_count]
        turned[common:] = upper_ref[(place_ref[1] + own_offset + y_count) % y_count]
        at_left = place_ref[0] == 0

        for part, (start, stop) in enumerate(bounds):
            far_ref, rest_ref = out_refs[2 * part : 2 * part + 2]
            for copy in copies[part]:
                copy.wait()

            def one(i, carry):
                local = pl.ds(pl.multiple_of(i * TILE_M, TILE_M), TILE_M)
                full = pl.ds(pl.multiple_of(start + i * TILE_M, TILE_M), TILE_M)
                tiles = [here[full]]
                if part == 0:
                    tiles.append(own_ref[local])
                depth_here = sum(tile.shape[1] for tile in tiles)
                total = jnp.dot(jnp.concatenate(tiles, axis=1), turned[:depth_here], preferred_element_type=jnp.float32)
                left, right = total[:, :width], total[:, width:]
                far_ref[local] = jnp.where(at_left, right, left)
                rest_ref[local] = stored_ref[full].astype(jnp.float32) - jnp.where(at_left, left, right)
                return carry

            lax.fori_loop(0, (stop - start) // TILE_M, one, 0)

    return pl.pallas_call(
        body,
        in_specs=[pl.BlockSpec(memory_space=pltpu.SMEM)]
        + [whole()] * 3
        + [pl.BlockSpec(memory_space=pltpu.HBM)] * len(blocks)
        + [whole()],
        out_specs=[whole()] * (2 * parts + 1),
        out_shape=[jax.ShapeDtypeStruct((b - a, width), jnp.float32) for a, b in bounds for _ in range(2)]
        + [jax.ShapeDtypeStruct((y_count, depth, both), stored.dtype)],
        scratch_shapes=[
            VM((common + depth, both), stored.dtype),
            VM((rows, common), stored.dtype),
            pltpu.SemaphoreType.DMA((parts * len(blocks),)),
        ],
        compiler_params=grant(48),
        name="early_products",
    )(place, got, twin, stored, *blocks, own_block)


def last_product(place, upper, base, offsets, blocks, bases, partner, out_dtype, sign):
    rows, width = base.shape
    y_count = upper.shape[0]

    def body(place_ref, upper_ref, base_ref, *refs):
        *block_refs, out_ref = refs
        side = (place_ref[0] + 1) % X_HI if partner else place_ref[0]
        columns = []
        for offset in offsets:
            both = upper_ref[(place_ref[1] + offset + y_count) % y_count]
            columns.append(jnp.where(side == 0, both[:, :width], both[:, width:]))
        columns = jnp.concatenate(columns, axis=0)
        for start in range(0, rows, TILE_M):
            part = slice(start, start + TILE_M)
            tiles = [ref[at + start : at + start + TILE_M] for ref, at in zip(block_refs, bases)]
            lhs = jnp.concatenate(tiles, axis=1)
            term = jnp.dot(lhs, columns, preferred_element_type=jnp.float32)
            out_ref[part] = (base_ref[part] + sign * term).astype(out_ref.dtype)

    return pl.pallas_call(
        body,
        in_specs=[pl.BlockSpec(memory_space=pltpu.SMEM)] + [whole()] * (2 + len(blocks)),
        out_specs=whole(),
        out_shape=jax.ShapeDtypeStruct((rows, width), out_dtype),
        compiler_params=grant(8),
        name="last_far" if partner else "last_own",
    )(place, upper, base, *blocks)


def per_device(slab_block, scale_first, scale_second, panel_lower):
    row_count, col_width = slab_block.shape
    chips = lax.axis_size("chip")
    groups = chips * CORES
    y_count = lax.axis_size("y")
    block_width = panel_lower.shape[1]
    share = row_count // groups

    up = [(i, (i + 1) % y_count) for i in range(y_count)]
    down = [(i, (i - 1) % y_count) for i in range(y_count)]
    route = {-1: up, 1: down}
    near = tuple(lax.ppermute(panel_lower, "y", route[sign]) for sign in route)

    first = (scale_first.astype(jnp.float32)[:, None] * slab_block.astype(jnp.float32)).astype(
        jnp.bfloat16
    )
    scale_rows = jnp.pad(
        jnp.transpose(scale_second.reshape(share, groups))[None], ((0, PAD - 1), (0, 0), (0, col_width - share))
    )
    packed = jnp.concatenate([first.reshape(share, groups, col_width), scale_rows], axis=0)
    packed = lax.all_to_all(packed, ROW, split_axis=1, concat_axis=0, tiled=True)
    joined = jnp.concatenate(near, axis=1)
    packed = after(packed, joined)
    far_near = tuple(lax.ppermute(block, "y", route[sign]) for block, sign in zip(near, route))
    bounds = ((0, SPLIT), (SPLIT, row_count))
    rising = [lax.ppermute(far_near[0][start:stop], "y", up) for start, stop in bounds]
    falling = lax.ppermute(far_near[1], "y", down)
    last = [lax.ppermute(rising[0], "y", up)]
    packed = packed.reshape(groups, share + PAD, col_width)
    top_count = PANEL_W // groups // X_HI
    stored, send = butterflies(packed, share, chips, top_count)
    got = lax.all_to_all(send, ("chip", "x_hi"), split_axis=0, concat_axis=0)
    twin = lax.ppermute(got, "core", [(0, 1), (1, 0)])
    place = jnp.stack([lax.axis_index(name) for name in ("x_hi", "y", "core")]).astype(jnp.int32)
    swap = [(i, X_HI - 1 - i) for i in range(X_HI)]
    *sums, upper = early_products(
        place,
        got,
        twin,
        stored,
        bounds,
        [0, -1, 1, -2, 2],
        [panel_lower, joined, *far_near],
        1 - y_count // 2,
        rising[0],
    )
    last.append(lax.ppermute(after(falling, upper)[SPLIT:], "y", down))
    out = []
    offsets = [y_count // 2 - 1, y_count // 2]
    for part, (start, _) in enumerate(bounds):
        blocks, bases, late = [falling, last[part]], [start, 0], []
        if part:
            blocks, bases, late = [*blocks, rising[part]], [*bases, 0], [1 - y_count // 2]
        far = last_product(place, upper, sums[2 * part], offsets + late, blocks, bases, True, jnp.bfloat16, 1)
        came = lax.ppermute(far, "x_hi", swap)
        rest = last_product(place, upper, sums[2 * part + 1], offsets + late, blocks, bases, False, jnp.float32, -1)
        out.append((rest - came.astype(jnp.float32)).astype(jnp.bfloat16))
    return jnp.concatenate(out, axis=0)


def solution(mesh):
    rows, cols = mesh.devices.shape
    split = Mesh(
        mesh.devices.reshape(rows // CORES, CORES, X_HI, cols // X_HI), ("chip", "core", "x_hi", "y")
    )
    col = ("x_hi", "y")
    placed = (P(ROW, col), P(ROW), P(ROW), P(ROW, col))
    return jax.shard_map(
        per_device, mesh=split, in_specs=placed, out_specs=P(ROW, col), check_vma=False
    )
```

```python
import jax
import jax.numpy as jnp
from jax import lax
from jax.experimental import pallas as pl
from jax.experimental.pallas import tpu as pltpu
from jax.sharding import Mesh, PartitionSpec as P

PANEL_W = 4096
X_HI = 2
CORES = 2
PAD = 8
TILE_M = 256
SPLIT = 1280
ROW = ("chip", "core")

inv_root = 0.7071067811865476


def after(value, *others):
    return lax.optimization_barrier((value, *others))[0]


VM = pltpu.VMEM


def grant(mib):
    return pltpu.CompilerParams(vmem_limit_bytes=mib << 20)


def whole():
    return pl.BlockSpec(memory_space=VM)


def butterflies(packed, share, chips, top_count):
    groups, _, width = packed.shape
    quarter = groups // 4
    rows = groups * share

    def body(packed_ref, stored_ref, send_ref):
        scale = jnp.transpose(packed_ref[:, share, :].astype(jnp.float32))
        for d in range(quarter):
            at = [d + n * quarter for n in range(4)]
            one = [packed_ref[n, :share].astype(jnp.float32) for n in at]
            two = [one[0] + one[2], one[1] + one[3], one[0] - one[2], one[1] - one[3]]
            two = [
                (scale[:share, n : n + 1] * (value * inv_root)).astype(packed.dtype).astype(jnp.float32)
                for n, value in zip(at, two)
            ]
            out = [two[0] + two[1], two[0] - two[1], two[2] + two[3], two[2] - two[3]]
            for n, value in zip(at, out):
                stored_ref[n * share : (n + 1) * share] = (value * inv_root).astype(packed.dtype)
        for x in range(X_HI):
            top = stored_ref[x * top_count : (x + 1) * top_count]
            for chip in range(chips):
                send_ref[chip * X_HI + x] = top

    return pl.pallas_call(
        body,
        in_specs=[whole()],
        out_specs=[whole(), whole()],
        out_shape=[
            jax.ShapeDtypeStruct((rows, width), packed.dtype),
            jax.ShapeDtypeStruct((chips * X_HI, top_count, width), packed.dtype),
        ],
        compiler_params=grant(8),
        name="butterflies",
    )(packed)


def order_upper(core, got_ref, twin_ref, out_ref):
    pairs, top, width = got_ref.shape
    y_count, depth = out_ref.shape[:2]
    chips, low = pairs // X_HI, top // y_count
    want = lax.broadcasted_iota(jnp.int32, (depth, depth), 0)
    have = lax.broadcasted_iota(jnp.int32, (depth, depth), 1)
    side = (want % CORES + core) % CORES
    source = side * (chips * low) + want // CORES % chips * low + want // (CORES * chips)
    move = jnp.where(source == have, 1.0, 0.0).astype(out_ref.dtype)
    for y in range(y_count):
        for x in range(X_HI):
            pick = [ref[chip * X_HI + x, y * low : (y + 1) * low] for ref in (got_ref, twin_ref) for chip in range(chips)]
            rows = jnp.dot(move, jnp.concatenate(pick, axis=0), preferred_element_type=jnp.float32)
            out_ref[y, :, x * width : (x + 1) * width] = rows.astype(out_ref.dtype)


def early_products(place, got, twin, stored, bounds, offsets, blocks, own_offset, own_block):
    rows, width = stored.shape
    y_count = lax.axis_size("y")
    depth, both = blocks[0].shape[1], X_HI * width
    parts = len(bounds)
    common = len(offsets) * depth
    starts = [sum(block.shape[1] for block in blocks[:n]) for n in range(len(blocks))]

    def body(place_ref, got_ref, twin_ref, stored_ref, *refs):
        block_refs, own_ref, out_refs = refs[: len(blocks)], refs[len(blocks)], refs[len(blocks) + 1 : -4]
        upper_ref, turned, here, arrived = refs[-4:]
        copies = [
            [
                pltpu.make_async_copy(
                    ref.at[start:stop], here.at[start:stop, at : at + ref.shape[1]], arrived.at[part * len(blocks) + n]
                )
                for n, (ref, at) in enumerate(zip(block_refs, starts))
            ]
            for part, (start, stop) in enumerate(bounds)
        ]
        for copy in sum(copies, []):
            copy.start()
        order_upper(place_ref[2], got_ref, twin_ref, upper_ref)
        for n, offset in enumerate(offsets):
            turned[n * depth : (n + 1) * depth] = upper_ref[(place_ref[1] + offset + y_count) % y_count]
        turned[common:] = upper_ref[(place_ref[1] + own_offset + y_count) % y_count]
        at_left = place_ref[0] == 0

        for part, (start, stop) in enumerate(bounds):
            far_ref, rest_ref = out_refs[2 * part : 2 * part + 2]
            for copy in copies[part]:
                copy.wait()

            def one(i, carry):
                local = pl.ds(pl.multiple_of(i * TILE_M, TILE_M), TILE_M)
                full = pl.ds(pl.multiple_of(start + i * TILE_M, TILE_M), TILE_M)
                tiles = [here[full]]
                if part == 0:
                    tiles.append(own_ref[local])
                depth_here = sum(tile.shape[1] for tile in tiles)
                total = jnp.dot(jnp.concatenate(tiles, axis=1), turned[:depth_here], preferred_element_type=jnp.float32)
                left, right = total[:, :width], total[:, width:]
                far_ref[local] = jnp.where(at_left, right, left)
                rest_ref[local] = stored_ref[full].astype(jnp.float32) - jnp.where(at_left, left, right)
                return carry

            lax.fori_loop(0, (stop - start) // TILE_M, one, 0)

    return pl.pallas_call(
        body,
        in_specs=[pl.BlockSpec(memory_space=pltpu.SMEM)]
        + [whole()] * 3
        + [pl.BlockSpec(memory_space=pltpu.HBM)] * len(blocks)
        + [whole()],
        out_specs=[whole()] * (2 * parts + 1),
        out_shape=[jax.ShapeDtypeStruct((b - a, width), jnp.float32) for a, b in bounds for _ in range(2)]
        + [jax.ShapeDtypeStruct((y_count, depth, both), stored.dtype)],
        scratch_shapes=[
            VM((common + depth, both), stored.dtype),
            VM((rows, common), stored.dtype),
            pltpu.SemaphoreType.DMA((parts * len(blocks),)),
        ],
        compiler_params=grant(48),
        name="early_products",
    )(place, got, twin, stored, *blocks, own_block)


def last_product(place, upper, base, offsets, blocks, bases, partner, out_dtype, sign):
    rows, width = base.shape
    y_count = upper.shape[0]

    def body(place_ref, upper_ref, base_ref, *refs):
        *block_refs, out_ref = refs
        side = (place_ref[0] + 1) % X_HI if partner else place_ref[0]
        columns = []
        for offset in offsets:
            both = upper_ref[(place_ref[1] + offset + y_count) % y_count]
            columns.append(jnp.where(side == 0, both[:, :width], both[:, width:]))
        columns = jnp.concatenate(columns, axis=0)
        for start in range(0, rows, TILE_M):
            part = slice(start, start + TILE_M)
            tiles = [ref[at + start : at + start + TILE_M] for ref, at in zip(block_refs, bases)]
            lhs = jnp.concatenate(tiles, axis=1)
            term = jnp.dot(lhs, columns, preferred_element_type=jnp.float32)
            out_ref[part] = (base_ref[part] + sign * term).astype(out_ref.dtype)

    return pl.pallas_call(
        body,
        in_specs=[pl.BlockSpec(memory_space=pltpu.SMEM)] + [whole()] * (2 + len(blocks)),
        out_specs=whole(),
        out_shape=jax.ShapeDtypeStruct((rows, width), out_dtype),
        compiler_params=grant(8),
        name="last_far" if partner else "last_own",
    )(place, upper, base, *blocks)


def per_device(slab_block, scale_first, scale_second, panel_lower):
    row_count, col_width = slab_block.shape
    chips = lax.axis_size("chip")
    groups = chips * CORES
    y_count = lax.axis_size("y")
    block_width = panel_lower.shape[1]
    share = row_count // groups

    up = [(i, (i + 1) % y_count) for i in range(y_count)]
    down = [(i, (i - 1) % y_count) for i in range(y_count)]
    route = {-1: up, 1: down}
    near = tuple(lax.ppermute(panel_lower, "y", route[sign]) for sign in route)

    first = (scale_first.astype(jnp.float32)[:, None] * slab_block.astype(jnp.float32)).astype(
        jnp.bfloat16
    )
    scale_rows = jnp.pad(
        jnp.transpose(scale_second.reshape(share, groups))[None], ((0, PAD - 1), (0, 0), (0, col_width - share))
    )
    packed = jnp.concatenate([first.reshape(share, groups, col_width), scale_rows], axis=0)
    packed = lax.all_to_all(packed, ROW, split_axis=1, concat_axis=0, tiled=True)
    joined = jnp.concatenate(near, axis=1)
    packed = after(packed, joined)
    far_near = tuple(lax.ppermute(block, "y", route[sign]) for block, sign in zip(near, route))
    bounds = ((0, SPLIT), (SPLIT, row_count))
    pieces = [far_near[0][start:stop] for start, stop in bounds]
    rising = [lax.ppermute(piece, "y", up) for piece in pieces]
    falling = lax.ppermute(far_near[1], "y", down)
    last = [lax.ppermute(after(rising[0], pieces[1]), "y", up)]
    packed = packed.reshape(groups, share + PAD, col_width)
    top_count = PANEL_W // groups // X_HI
    stored, send = butterflies(packed, share, chips, top_count)
    got = lax.all_to_all(send, ("chip", "x_hi"), split_axis=0, concat_axis=0)
    twin = lax.ppermute(got, "core", [(0, 1), (1, 0)])
    place = jnp.stack([lax.axis_index(name) for name in ("x_hi", "y", "core")]).astype(jnp.int32)
    swap = [(i, X_HI - 1 - i) for i in range(X_HI)]
    *sums, upper = early_products(
        place,
        got,
        twin,
        stored,
        bounds,
        [0, -1, 1, -2, 2],
        [panel_lower, joined, *far_near],
        1 - y_count // 2,
        rising[0],
    )
    last.append(lax.ppermute(after(falling, upper)[SPLIT:], "y", down))
    offsets = [y_count // 2 - 1, y_count // 2]
    late = [(offsets, [falling, last[0]], [0, 0])]
    late.append(([*offsets, 1 - y_count // 2], [falling, last[1], rising[1]], [SPLIT, 0, 0]))
    fars = [
        last_product(place, upper, sums[2 * part], *args, True, jnp.bfloat16, 1) for part, args in enumerate(late)
    ]
    out = []
    for part, args in enumerate(late):
        came = lax.ppermute(fars[part], "x_hi", swap)
        base = after(sums[2 * part + 1], fars[-1])
        rest = last_product(place, upper, base, *args, False, jnp.float32, -1)
        out.append((rest - came.astype(jnp.float32)).astype(jnp.bfloat16))
    return jnp.concatenate(out, axis=0)


def solution(mesh):
    rows, cols = mesh.devices.shape
    split = Mesh(
        mesh.devices.reshape(rows // CORES, CORES, X_HI, cols // X_HI), ("chip", "core", "x_hi", "y")
    )
    col = ("x_hi", "y")
    placed = (P(ROW, col), P(ROW), P(ROW), P(ROW, col))
    return jax.shard_map(
        per_device, mesh=split, in_specs=placed, out_specs=P(ROW, col), check_vma=False
    )
```

```python
import jax
import jax.numpy as jnp
from jax import lax
from jax.experimental import pallas as pl
from jax.experimental.pallas import tpu as pltpu
from jax.sharding import Mesh, PartitionSpec as P

PANEL_W = 4096
X_HI = 2
CORES = 2
PAD = 8
TILE_M = 256
SPLIT = 1280
ROW = ("chip", "core")

inv_root = 0.7071067811865476


def after(value, *others):
    return lax.optimization_barrier((value, *others))[0]


VM = pltpu.VMEM


def grant(mib):
    return pltpu.CompilerParams(vmem_limit_bytes=mib << 20)


def whole():
    return pl.BlockSpec(memory_space=VM)


def butterflies(packed, share, chips, top_count):
    groups, _, width = packed.shape
    quarter = groups // 4
    rows = groups * share

    def body(packed_ref, stored_ref, send_ref):
        scale = jnp.transpose(packed_ref[:, share, :].astype(jnp.float32))
        for d in range(quarter):
            at = [d + n * quarter for n in range(4)]
            one = [packed_ref[n, :share].astype(jnp.float32) for n in at]
            two = [one[0] + one[2], one[1] + one[3], one[0] - one[2], one[1] - one[3]]
            two = [
                (scale[:share, n : n + 1] * (value * inv_root)).astype(packed.dtype).astype(jnp.float32)
                for n, value in zip(at, two)
            ]
            out = [two[0] + two[1], two[0] - two[1], two[2] + two[3], two[2] - two[3]]
            for n, value in zip(at, out):
                stored_ref[n * share : (n + 1) * share] = (value * inv_root).astype(packed.dtype)
        for x in range(X_HI):
            top = stored_ref[x * top_count : (x + 1) * top_count]
            for chip in range(chips):
                send_ref[chip * X_HI + x] = top

    return pl.pallas_call(
        body,
        in_specs=[whole()],
        out_specs=[whole(), whole()],
        out_shape=[
            jax.ShapeDtypeStruct((rows, width), packed.dtype),
            jax.ShapeDtypeStruct((chips * X_HI, top_count, width), packed.dtype),
        ],
        compiler_params=grant(8),
        name="butterflies",
    )(packed)


def order_upper(core, got_ref, twin_ref, out_ref):
    pairs, top, width = got_ref.shape
    y_count, depth = out_ref.shape[:2]
    chips, low = pairs // X_HI, top // y_count
    want = lax.broadcasted_iota(jnp.int32, (depth, depth), 0)
    have = lax.broadcasted_iota(jnp.int32, (depth, depth), 1)
    side = (want % CORES + core) % CORES
    source = side * (chips * low) + want // CORES % chips * low + want // (CORES * chips)
    move = jnp.where(source == have, 1.0, 0.0).astype(out_ref.dtype)
    for y in range(y_count):
        for x in range(X_HI):
            pick = [ref[chip * X_HI + x, y * low : (y + 1) * low] for ref in (got_ref, twin_ref) for chip in range(chips)]
            rows = jnp.dot(move, jnp.concatenate(pick, axis=0), preferred_element_type=jnp.float32)
            out_ref[y, :, x * width : (x + 1) * width] = rows.astype(out_ref.dtype)


def early_products(place, got, twin, stored, bounds, offsets, blocks, own_offset, own_block):
    rows, width = stored.shape
    y_count = lax.axis_size("y")
    depth, both = blocks[0].shape[1], X_HI * width
    parts = len(bounds)
    common = len(offsets) * depth
    starts = [sum(block.shape[1] for block in blocks[:n]) for n in range(len(blocks))]

    def body(place_ref, got_ref, twin_ref, stored_ref, *refs):
        block_refs, own_ref, out_refs = refs[: len(blocks)], refs[len(blocks)], refs[len(blocks) + 1 : -4]
        upper_ref, turned, here, arrived = refs[-4:]
        copies = [
            [
                pltpu.make_async_copy(
                    ref.at[start:stop], here.at[start:stop, at : at + ref.shape[1]], arrived.at[part * len(blocks) + n]
                )
                for n, (ref, at) in enumerate(zip(block_refs, starts))
            ]
            for part, (start, stop) in enumerate(bounds)
        ]
        for copy in sum(copies, []):
            copy.start()
        order_upper(place_ref[2], got_ref, twin_ref, upper_ref)
        for n, offset in enumerate(offsets):
            turned[n * depth : (n + 1) * depth] = upper_ref[(place_ref[1] + offset + y_count) % y_count]
        turned[common:] = upper_ref[(place_ref[1] + own_offset + y_count) % y_count]
        at_left = place_ref[0] == 0

        for part, (start, stop) in enumerate(bounds):
            far_ref, rest_ref = out_refs[2 * part : 2 * part + 2]
            for copy in copies[part]:
                copy.wait()

            def one(i, carry):
                local = pl.ds(pl.multiple_of(i * TILE_M, TILE_M), TILE_M)
                full = pl.ds(pl.multiple_of(start + i * TILE_M, TILE_M), TILE_M)
                tiles = [here[full]]
                if part == 0:
                    tiles.append(own_ref[local])
                depth_here = sum(tile.shape[1] for tile in tiles)
                total = jnp.dot(jnp.concatenate(tiles, axis=1), turned[:depth_here], preferred_element_type=jnp.float32)
                left, right = total[:, :width], total[:, width:]
                far_ref[local] = jnp.where(at_left, right, left)
                rest_ref[local] = stored_ref[full].astype(jnp.float32) - jnp.where(at_left, left, right)
                return carry

            lax.fori_loop(0, (stop - start) // TILE_M, one, 0, unroll=True)

    return pl.pallas_call(
        body,
        in_specs=[pl.BlockSpec(memory_space=pltpu.SMEM)]
        + [whole()] * 3
        + [pl.BlockSpec(memory_space=pltpu.HBM)] * len(blocks)
        + [whole()],
        out_specs=[whole()] * (2 * parts + 1),
        out_shape=[jax.ShapeDtypeStruct((b - a, width), jnp.float32) for a, b in bounds for _ in range(2)]
        + [jax.ShapeDtypeStruct((y_count, depth, both), stored.dtype)],
        scratch_shapes=[
            VM((common + depth, both), stored.dtype),
            VM((rows, common), stored.dtype),
            pltpu.SemaphoreType.DMA((parts * len(blocks),)),
        ],
        compiler_params=grant(48),
        name="early_products",
    )(place, got, twin, stored, *blocks, own_block)


def last_product(place, upper, base, offsets, blocks, bases, partner, out_dtype, sign):
    rows, width = base.shape
    y_count = upper.shape[0]

    def body(place_ref, upper_ref, base_ref, *refs):
        *block_refs, out_ref = refs
        side = (place_ref[0] + 1) % X_HI if partner else place_ref[0]
        columns = []
        for offset in offsets:
            both = upper_ref[(place_ref[1] + offset + y_count) % y_count]
            columns.append(jnp.where(side == 0, both[:, :width], both[:, width:]))
        columns = jnp.concatenate(columns, axis=0)
        for start in range(0, rows, TILE_M):
            part = slice(start, start + TILE_M)
            tiles = [ref[at + start : at + start + TILE_M] for ref, at in zip(block_refs, bases)]
            lhs = jnp.concatenate(tiles, axis=1)
            term = jnp.dot(lhs, columns, preferred_element_type=jnp.float32)
            out_ref[part] = (base_ref[part] + sign * term).astype(out_ref.dtype)

    return pl.pallas_call(
        body,
        in_specs=[pl.BlockSpec(memory_space=pltpu.SMEM)] + [whole()] * (2 + len(blocks)),
        out_specs=whole(),
        out_shape=jax.ShapeDtypeStruct((rows, width), out_dtype),
        compiler_params=grant(8),
        name="last_far" if partner else "last_own",
    )(place, upper, base, *blocks)


def per_device(slab_block, scale_first, scale_second, panel_lower):
    row_count, col_width = slab_block.shape
    chips = lax.axis_size("chip")
    groups = chips * CORES
    y_count = lax.axis_size("y")
    block_width = panel_lower.shape[1]
    share = row_count // groups

    up = [(i, (i + 1) % y_count) for i in range(y_count)]
    down = [(i, (i - 1) % y_count) for i in range(y_count)]
    route = {-1: up, 1: down}
    near = tuple(lax.ppermute(panel_lower, "y", route[sign]) for sign in route)

    first = (scale_first.astype(jnp.float32)[:, None] * slab_block.astype(jnp.float32)).astype(
        jnp.bfloat16
    )
    scale_rows = jnp.pad(
        jnp.transpose(scale_second.reshape(share, groups))[None], ((0, PAD - 1), (0, 0), (0, col_width - share))
    )
    packed = jnp.concatenate([first.reshape(share, groups, col_width), scale_rows], axis=0)
    packed = lax.all_to_all(packed, ROW, split_axis=1, concat_axis=0, tiled=True)
    joined = jnp.concatenate(near, axis=1)
    packed = after(packed, joined)
    far_near = tuple(lax.ppermute(block, "y", route[sign]) for block, sign in zip(near, route))
    bounds = ((0, SPLIT), (SPLIT, row_count))
    pieces = [far_near[0][start:stop] for start, stop in bounds]
    rising = [lax.ppermute(piece, "y", up) for piece in pieces]
    falling = lax.ppermute(far_near[1], "y", down)
    last = [lax.ppermute(after(rising[0], pieces[1]), "y", up)]
    packed = packed.reshape(groups, share + PAD, col_width)
    top_count = PANEL_W // groups // X_HI
    stored, send = butterflies(packed, share, chips, top_count)
    got = lax.all_to_all(send, ("chip", "x_hi"), split_axis=0, concat_axis=0)
    twin = lax.ppermute(got, "core", [(0, 1), (1, 0)])
    place = jnp.stack([lax.axis_index(name) for name in ("x_hi", "y", "core")]).astype(jnp.int32)
    swap = [(i, X_HI - 1 - i) for i in range(X_HI)]
    *sums, upper = early_products(
        place,
        got,
        twin,
        stored,
        bounds,
        [0, -1, 1, -2, 2],
        [panel_lower, joined, *far_near],
        1 - y_count // 2,
        rising[0],
    )
    last.append(lax.ppermute(after(falling, upper)[SPLIT:], "y", down))
    offsets = [y_count // 2 - 1, y_count // 2]
    late = [(offsets, [falling, last[0]], [0, 0])]
    late.append(([*offsets, 1 - y_count // 2], [falling, last[1], rising[1]], [SPLIT, 0, 0]))
    fars = [
        last_product(place, upper, sums[2 * part], *args, True, jnp.bfloat16, 1) for part, args in enumerate(late)
    ]
    out = []
    for part, args in enumerate(late):
        came = lax.ppermute(fars[part], "x_hi", swap)
        base = after(sums[2 * part + 1], fars[-1])
        rest = last_product(place, upper, base, *args, False, jnp.float32, -1)
        out.append((rest - came.astype(jnp.float32)).astype(jnp.bfloat16))
    return jnp.concatenate(out, axis=0)


def solution(mesh):
    rows, cols = mesh.devices.shape
    split = Mesh(
        mesh.devices.reshape(rows // CORES, CORES, X_HI, cols // X_HI), ("chip", "core", "x_hi", "y")
    )
    col = ("x_hi", "y")
    placed = (P(ROW, col), P(ROW), P(ROW), P(ROW, col))
    return jax.shard_map(
        per_device, mesh=split, in_specs=placed, out_specs=P(ROW, col), check_vma=False
    )
```

```python
import jax
import jax.numpy as jnp
from jax import lax
from jax.experimental import pallas as pl
from jax.experimental.pallas import tpu as pltpu
from jax.sharding import Mesh, PartitionSpec as P

PANEL_W = 4096
X_HI = 2
CORES = 2
PAD = 8
TILE_M = 128
SPLIT = 1280
ROW = ("chip", "core")

inv_root = 0.7071067811865476


def after(value, *others):
    return lax.optimization_barrier((value, *others))[0]


VM = pltpu.VMEM


def grant(mib):
    return pltpu.CompilerParams(vmem_limit_bytes=mib << 20)


def whole():
    return pl.BlockSpec(memory_space=VM)


def butterflies(packed, share, chips, top_count):
    groups, _, width = packed.shape
    quarter = groups // 4
    rows = groups * share

    def body(packed_ref, stored_ref, send_ref):
        scale = jnp.transpose(packed_ref[:, share, :].astype(jnp.float32))
        for d in range(quarter):
            at = [d + n * quarter for n in range(4)]
            one = [packed_ref[n, :share].astype(jnp.float32) for n in at]
            two = [one[0] + one[2], one[1] + one[3], one[0] - one[2], one[1] - one[3]]
            two = [
                (scale[:share, n : n + 1] * (value * inv_root)).astype(packed.dtype).astype(jnp.float32)
                for n, value in zip(at, two)
            ]
            out = [two[0] + two[1], two[0] - two[1], two[2] + two[3], two[2] - two[3]]
            for n, value in zip(at, out):
                stored_ref[n * share : (n + 1) * share] = (value * inv_root).astype(packed.dtype)
        for x in range(X_HI):
            top = stored_ref[x * top_count : (x + 1) * top_count]
            for chip in range(chips):
                send_ref[chip * X_HI + x] = top

    return pl.pallas_call(
        body,
        in_specs=[whole()],
        out_specs=[whole(), whole()],
        out_shape=[
            jax.ShapeDtypeStruct((rows, width), packed.dtype),
            jax.ShapeDtypeStruct((chips * X_HI, top_count, width), packed.dtype),
        ],
        compiler_params=grant(8),
        name="butterflies",
    )(packed)


def order_upper(core, got_ref, twin_ref, out_ref):
    pairs, top, width = got_ref.shape
    y_count, depth = out_ref.shape[:2]
    chips, low = pairs // X_HI, top // y_count
    want = lax.broadcasted_iota(jnp.int32, (depth, depth), 0)
    have = lax.broadcasted_iota(jnp.int32, (depth, depth), 1)
    side = (want % CORES + core) % CORES
    source = side * (chips * low) + want // CORES % chips * low + want // (CORES * chips)
    move = jnp.where(source == have, 1.0, 0.0).astype(out_ref.dtype)
    for y in range(y_count):
        for x in range(X_HI):
            pick = [ref[chip * X_HI + x, y * low : (y + 1) * low] for ref in (got_ref, twin_ref) for chip in range(chips)]
            rows = jnp.dot(move, jnp.concatenate(pick, axis=0), preferred_element_type=jnp.float32)
            out_ref[y, :, x * width : (x + 1) * width] = rows.astype(out_ref.dtype)


def early_products(place, got, twin, stored, bounds, offsets, blocks, own_offset, own_block):
    rows, width = stored.shape
    y_count = lax.axis_size("y")
    depth, both = blocks[0].shape[1], X_HI * width
    parts = len(bounds)
    common = len(offsets) * depth
    starts = [sum(block.shape[1] for block in blocks[:n]) for n in range(len(blocks))]

    def body(place_ref, got_ref, twin_ref, stored_ref, *refs):
        block_refs, own_ref, out_refs = refs[: len(blocks)], refs[len(blocks)], refs[len(blocks) + 1 : -4]
        upper_ref, turned, here, arrived = refs[-4:]
        copies = [
            [
                pltpu.make_async_copy(
                    ref.at[start:stop], here.at[start:stop, at : at + ref.shape[1]], arrived.at[part * len(blocks) + n]
                )
                for n, (ref, at) in enumerate(zip(block_refs, starts))
            ]
            for part, (start, stop) in enumerate(bounds)
        ]
        for copy in sum(copies, []):
            copy.start()
        order_upper(place_ref[2], got_ref, twin_ref, upper_ref)
        for n, offset in enumerate(offsets):
            turned[n * depth : (n + 1) * depth] = upper_ref[(place_ref[1] + offset + y_count) % y_count]
        turned[common:] = upper_ref[(place_ref[1] + own_offset + y_count) % y_count]
        at_left = place_ref[0] == 0

        for part, (start, stop) in enumerate(bounds):
            far_ref, rest_ref = out_refs[2 * part : 2 * part + 2]
            for copy in copies[part]:
                copy.wait()

            def one(i, carry):
                local = pl.ds(pl.multiple_of(i * TILE_M, TILE_M), TILE_M)
                full = pl.ds(pl.multiple_of(start + i * TILE_M, TILE_M), TILE_M)
                tiles = [here[full]]
                if part == 0:
                    tiles.append(own_ref[local])
                depth_here = sum(tile.shape[1] for tile in tiles)
                total = jnp.dot(jnp.concatenate(tiles, axis=1), turned[:depth_here], preferred_element_type=jnp.float32)
                left, right = total[:, :width], total[:, width:]
                far_ref[local] = jnp.where(at_left, right, left)
                rest_ref[local] = stored_ref[full].astype(jnp.float32) - jnp.where(at_left, left, right)
                return carry

            lax.fori_loop(0, (stop - start) // TILE_M, one, 0, unroll=True)

    return pl.pallas_call(
        body,
        in_specs=[pl.BlockSpec(memory_space=pltpu.SMEM)]
        + [whole()] * 3
        + [pl.BlockSpec(memory_space=pltpu.HBM)] * len(blocks)
        + [whole()],
        out_specs=[whole()] * (2 * parts + 1),
        out_shape=[jax.ShapeDtypeStruct((b - a, width), jnp.float32) for a, b in bounds for _ in range(2)]
        + [jax.ShapeDtypeStruct((y_count, depth, both), stored.dtype)],
        scratch_shapes=[
            VM((common + depth, both), stored.dtype),
            VM((rows, common), stored.dtype),
            pltpu.SemaphoreType.DMA((parts * len(blocks),)),
        ],
        compiler_params=grant(48),
        name="early_products",
    )(place, got, twin, stored, *blocks, own_block)


def last_product(place, upper, base, offsets, blocks, bases, partner, out_dtype, sign):
    rows, width = base.shape
    y_count = upper.shape[0]

    def body(place_ref, upper_ref, base_ref, *refs):
        *block_refs, out_ref = refs
        side = (place_ref[0] + 1) % X_HI if partner else place_ref[0]
        columns = []
        for offset in offsets:
            both = upper_ref[(place_ref[1] + offset + y_count) % y_count]
            columns.append(jnp.where(side == 0, both[:, :width], both[:, width:]))
        columns = jnp.concatenate(columns, axis=0)
        for start in range(0, rows, TILE_M):
            part = slice(start, start + TILE_M)
            tiles = [ref[at + start : at + start + TILE_M] for ref, at in zip(block_refs, bases)]
            lhs = jnp.concatenate(tiles, axis=1)
            term = jnp.dot(lhs, columns, preferred_element_type=jnp.float32)
            out_ref[part] = (base_ref[part] + sign * term).astype(out_ref.dtype)

    return pl.pallas_call(
        body,
        in_specs=[pl.BlockSpec(memory_space=pltpu.SMEM)] + [whole()] * (2 + len(blocks)),
        out_specs=whole(),
        out_shape=jax.ShapeDtypeStruct((rows, width), out_dtype),
        compiler_params=grant(8),
        name="last_far" if partner else "last_own",
    )(place, upper, base, *blocks)


def per_device(slab_block, scale_first, scale_second, panel_lower):
    row_count, col_width = slab_block.shape
    chips = lax.axis_size("chip")
    groups = chips * CORES
    y_count = lax.axis_size("y")
    block_width = panel_lower.shape[1]
    share = row_count // groups

    up = [(i, (i + 1) % y_count) for i in range(y_count)]
    down = [(i, (i - 1) % y_count) for i in range(y_count)]
    route = {-1: up, 1: down}
    near = tuple(lax.ppermute(panel_lower, "y", route[sign]) for sign in route)

    first = (scale_first.astype(jnp.float32)[:, None] * slab_block.astype(jnp.float32)).astype(
        jnp.bfloat16
    )
    scale_rows = jnp.pad(
        jnp.transpose(scale_second.reshape(share, groups))[None], ((0, PAD - 1), (0, 0), (0, col_width - share))
    )
    packed = jnp.concatenate([first.reshape(share, groups, col_width), scale_rows], axis=0)
    packed = lax.all_to_all(packed, ROW, split_axis=1, concat_axis=0, tiled=True)
    joined = jnp.concatenate(near, axis=1)
    packed = after(packed, joined)
    far_near = tuple(lax.ppermute(block, "y", route[sign]) for block, sign in zip(near, route))
    bounds = ((0, SPLIT), (SPLIT, row_count))
    pieces = [far_near[0][start:stop] for start, stop in bounds]
    rising = [lax.ppermute(piece, "y", up) for piece in pieces]
    falling = lax.ppermute(far_near[1], "y", down)
    last = [lax.ppermute(after(rising[0], pieces[1]), "y", up)]
    packed = packed.reshape(groups, share + PAD, col_width)
    top_count = PANEL_W // groups // X_HI
    stored, send = butterflies(packed, share, chips, top_count)
    got = lax.all_to_all(send, ("chip", "x_hi"), split_axis=0, concat_axis=0)
    twin = lax.ppermute(got, "core", [(0, 1), (1, 0)])
    place = jnp.stack([lax.axis_index(name) for name in ("x_hi", "y", "core")]).astype(jnp.int32)
    swap = [(i, X_HI - 1 - i) for i in range(X_HI)]
    *sums, upper = early_products(
        place,
        got,
        twin,
        stored,
        bounds,
        [0, -1, 1, -2, 2],
        [panel_lower, joined, *far_near],
        1 - y_count // 2,
        rising[0],
    )
    last.append(lax.ppermute(after(falling, upper)[SPLIT:], "y", down))
    offsets = [y_count // 2 - 1, y_count // 2]
    late = [(offsets, [falling, last[0]], [0, 0])]
    late.append(([*offsets, 1 - y_count // 2], [falling, last[1], rising[1]], [SPLIT, 0, 0]))
    fars = [
        last_product(place, upper, sums[2 * part], *args, True, jnp.bfloat16, 1) for part, args in enumerate(late)
    ]
    out = []
    for part, args in enumerate(late):
        came = lax.ppermute(fars[part], "x_hi", swap)
        base = after(sums[2 * part + 1], fars[-1])
        rest = last_product(place, upper, base, *args, False, jnp.float32, -1)
        out.append((rest - came.astype(jnp.float32)).astype(jnp.bfloat16))
    return jnp.concatenate(out, axis=0)


def solution(mesh):
    rows, cols = mesh.devices.shape
    split = Mesh(
        mesh.devices.reshape(rows // CORES, CORES, X_HI, cols // X_HI), ("chip", "core", "x_hi", "y")
    )
    col = ("x_hi", "y")
    placed = (P(ROW, col), P(ROW), P(ROW), P(ROW, col))
    return jax.shard_map(
        per_device, mesh=split, in_specs=placed, out_specs=P(ROW, col), check_vma=False
    )
```
